256 devices in a mesh: seq: 32 (over z, y), grp: 8 (over x, core).
Axes of the slice: x: 4, y: 4, z: 8, core: 2. Of those that a mesh axis runs over, the one named last changes fastest.
Arguments:
- x_in: bfloat16 [4096, 8192], P('seq', 'grp'), may hold values from -6 to 6
- multiplier_channels: bfloat16 [4096, 8192], P('seq', 'grp'), may hold values from -6 to 6
- b_proj: bfloat16 [4096, 1024], P('seq', 'grp'), may hold values from -6 to 6
- c_proj: bfloat16 [4096, 1024], P('seq', 'grp'), may hold values from -0.5 to 0.5
- dt_raw: float32 [4096, 64], P('seq', 'grp'), as said below
- dt_bias: float32 [64], P('grp'), may hold values from -3.5 to -1.5
- a_log: float32 [64], P('grp'), as said below
- skip_d: float32 [64], P('grp'), may hold values from 0.2 to 1
- norm_gain: float32 [8192], P('grp'), may hold values from 0.5 to 1.5
- w_out: bfloat16 [8192, 8192], P('grp', 'seq'), may hold values from -0.03125 to 0.03125
Outputs:
- mixed: bfloat16 [4096, 8192], P('seq', 'grp')
The draws below stay inside these ranges and needn't reach their ends.
Inputs may be any that keep to these rules, and one draw needn't show every extreme that they name: `dt_raw`: step size offsets, with bursts at a few positions of the sequence shared by all heads. `a_log`: log decay rates per head, between log(0.1 / (0.08 * 4096)) and log(0.6).
All inputs are finite; a program needn't handle non-finite values.
Results may differ from the reference program's by a relative error of at most 0.0049.
Values may be sent and summed in bfloat16 or wider, within the bound.
A program may use at most 128 MiB of HBM per device.

```python
import math
import jax
import jax.numpy as jnp
from jax import lax

D_MODEL = 8192
HEADS = 64
CHANNEL_WIDTH = 128
STATE = 128
HEAD_GROUPS = 8
TOK_DEV = 128
LENGTH_OF_TEXT = 4096


def draw_a_log(key, part):
    first, latter_portion, third = jax.random.split(jax.random.fold_in(key, 11), 3)
    share = 0.5
    slow = jax.random.uniform(first, (HEADS,), jnp.float32) < share
    slow_rate = jnp.exp(jax.random.uniform(latter_portion, (HEADS,), jnp.float32, math.log(0.1), math.log(1.0))) / (0.08 * LENGTH_OF_TEXT)
    fast_rate = jnp.exp(jax.random.uniform(third, (HEADS,), jnp.float32, math.log(0.06), math.log(0.6)))
    return jnp.log(jnp.where(slow, slow_rate, fast_rate)).astype(jnp.float32)


def draw_dt_raw(key, part):
    first, latter_portion, third = jax.random.split(jax.random.fold_in(key, 23), 3)
    shift_start_index = 0.5 * jax.random.normal(first, (LENGTH_OF_TEXT, HEADS), jnp.float32)
    block_count = LENGTH_OF_TEXT // TOK_DEV
    block_shift = jax.random.uniform(third, (block_count, HEADS), jnp.float32, -1.5, 1.5)
    block_shift = jnp.repeat(block_shift, TOK_DEV, axis=0)
    position_spans = jax.random.uniform(latter_portion, (LENGTH_OF_TEXT, 1), jnp.float32) < 6.0 / LENGTH_OF_TEXT
    base_values = shift_start_index + block_shift
    return jnp.where(position_spans, 3.0 + base_values, base_values).astype(jnp.float32)


def levels(rng, dims, pieces, low, largest):
    def one(position, shards_of):
        heights = jax.random.uniform(jax.random.fold_in(jax.random.fold_in(rng, 6), position), (shards_of,), jnp.float32, low / len(pieces), largest / len(pieces))
        return jnp.repeat(jnp.exp(heights), dims[position] // shards_of).reshape((-1,) + (1,) * (len(dims) - position - 1))

    loudness = one(*pieces[0])
    for cut in pieces[1:]:
        loudness = loudness * one(*cut)
    return loudness


def centred(key, dims, scale, bound, cuts=(), held_as=jnp.bfloat16):
    gain = levels(key, dims, cuts, -0.22, 0.18) if cuts else 1.0
    array = jax.random.normal(key, dims, jnp.float32) * scale * gain
    return jnp.minimum(jnp.maximum(array, -bound), bound).astype(held_as)


def setup_inputs(seed: int = 0) -> dict:
    arg_keys = jax.random.split(jax.random.key(seed), 11)
    return {
        "x_in": centred(arg_keys[0], (LENGTH_OF_TEXT, HEADS * CHANNEL_WIDTH), 1.0, 6.0, ((0, 32), (1, 8))),
        "multiplier_channels": centred(arg_keys[1], (LENGTH_OF_TEXT, HEADS * CHANNEL_WIDTH), 1.0, 6.0, ((0, 32), (1, 8))),
        "b_proj": centred(arg_keys[2], (LENGTH_OF_TEXT, HEAD_GROUPS * STATE), 1.0, 6.0, ((0, 32), (1, 8))),
        "c_proj": centred(arg_keys[3], (LENGTH_OF_TEXT, HEAD_GROUPS * STATE), STATE ** -0.5, 0.5, ((0, 32), (1, 8))),
        "dt_raw": draw_dt_raw(jax.random.fold_in(arg_keys[10], 71), 0),
        "dt_bias": jnp.clip(-3.5 + 2.0 * jax.random.uniform(arg_keys[5], (HEADS,), jnp.float32) ** levels(arg_keys[5], (HEADS,), ((0, 8),), -0.2, 0.2), -3.5, -1.5),
        "a_log": draw_a_log(jax.random.fold_in(arg_keys[10], 71), 0),
        "skip_d": jnp.clip(0.2 + 0.8 * jax.random.uniform(arg_keys[7], (HEADS,), jnp.float32) ** levels(arg_keys[7], (HEADS,), ((0, 8),), -0.2, 0.2), 0.2, 1.0),
        "norm_gain": jnp.clip(1.0 + 0.1 * jax.random.normal(arg_keys[8], (HEADS * CHANNEL_WIDTH,), jnp.float32), 0.5, 1.5),
        "w_out": centred(arg_keys[9], (HEADS * CHANNEL_WIDTH, D_MODEL), (4 * HEADS * CHANNEL_WIDTH) ** -0.5, 0.03125, ((0, 8), (1, 32))),
    }


HIGH = lax.Precision.HIGHEST

def ssd_blocks(xf, dt, la, bm, cm, init):
    length, heads, width = xf.shape
    groups = bm.shape[1]
    ratio = heads // groups
    block = math.gcd(length, 256)
    count = length // block

    def step(state, blk):
        xb, dtb, lab, bb, cb = blk
        cum = jnp.cumsum(lab, axis=0)
        attention_logits = jnp.einsum('tgn,sgn->gts', cb, bb, precision=HIGH)
        attention_logits = jnp.repeat(attention_logits, ratio, axis=0)
        diff = cum.T[:, :, None] - cum.T[:, None, :]
        rows = lax.broadcasted_iota(jnp.int32, (block, block), 0)
        cols = lax.broadcasted_iota(jnp.int32, (block, block), 1)
        mask = (rows >= cols)[None, :, :]
        decay = jnp.exp(jnp.where(mask, diff, -1e+30))
        mixing = decay * attention_logits * dtb.T[:, None, :]
        outs = jnp.einsum('hts,shp->thp', mixing, xb, precision=HIGH)
        cheads = jnp.repeat(cb, ratio, axis=1)
        incoming_channel_bundles = jnp.repeat(bb, ratio, axis=1)
        outs = outs + jnp.exp(cum)[:, :, None] * jnp.einsum('thn,hpn->thp', cheads, state, precision=HIGH)
        weights = jnp.exp(cum[-1][None, :] - cum) * dtb
        fresh = jnp.einsum('sh,shp,shn->hpn', weights, xb, incoming_channel_bundles, precision=HIGH)
        state = jnp.exp(cum[-1])[:, None, None] * state + fresh
        return (state, outs)
    blocks = (xf.reshape(count, block, heads, width), dt.reshape(count, block, heads), la.reshape(count, block, heads), bm.reshape(count, block, groups, -1), cm.reshape(count, block, groups, -1))
    final, outs = lax.scan(step, init, blocks)
    return (outs.reshape(length, heads, width), final, lax.optimization_barrier(jnp.sum(la, axis=0)))

def gated_norm_output(y, multiplier_channels, norm_gain, groups):
    length = y.shape[0]
    gated = y.reshape(length, -1) * jax.nn.silu(multiplier_channels.astype(jnp.float32))
    split = gated.reshape(length, groups, -1)
    split = split * lax.rsqrt(lax.optimization_barrier(jnp.mean(split * split, axis=-1, keepdims=True)) + 1e-05)
    return (split.reshape(length, -1) * norm_gain).astype(jnp.bfloat16)

def reference(x_in, multiplier_channels, b_proj, c_proj, dt_raw, dt_bias, a_log, skip_d, norm_gain, w_out):
    length = x_in.shape[0]
    xf = x_in.astype(jnp.float32).reshape(length, HEADS, CHANNEL_WIDTH)
    dt = jax.nn.softplus(dt_raw + dt_bias)
    la = -jnp.exp(a_log) * dt
    bm = b_proj.astype(jnp.float32).reshape(length, HEAD_GROUPS, STATE)
    cm = c_proj.astype(jnp.float32).reshape(length, HEAD_GROUPS, STATE)
    init = jnp.zeros((HEADS, CHANNEL_WIDTH, STATE), jnp.float32)
    y, final, total = ssd_blocks(xf, dt, la, bm, cm, init)
    y = y + skip_d[None, :, None] * xf
    normed = gated_norm_output(y, multiplier_channels, norm_gain, HEAD_GROUPS)
    return jnp.dot(normed, w_out, preferred_element_type=jnp.float32).astype(jnp.bfloat16)
```

```python
import jax
import jax.numpy as jnp
from jax import lax
from jax.experimental import pallas as pl
from jax.experimental.pallas import tpu as pltpu
from jax.sharding import PartitionSpec as P

MESH = pl.DeviceIdType.MESH
HIGH = lax.Precision.HIGHEST
WIDTH = 128
STATE = 128
NZ, NY, NX, NC = 8, 4, 4, 2
F32 = jnp.float32
BF16 = jnp.bfloat16


def split(value):
    high = value.astype(BF16)
    return high, (value - high.astype(F32)).astype(BF16)


def dot(a, b, dims=((1,), (0,))):
    return lax.dot_general(a, b, (dims, ((), ())), preferred_element_type=F32)


def kernel(
    x_ref, m_ref, b_ref, c_ref, dt_ref, bias_ref, alog_ref, skip_ref, gain_ref, w_ref,
    out_ref,
    wall, abuf, ybuf, smbuf, qbuf,
    lsend, lrecv, tsend, trecv,
    rsend, rrecv, dsend, drecv,
    esend, erecv, ssend, srecv,
    psend, precv, keep, rssend, rsrecv, fsend,
    w_local, w_ss, w_rs, l_ss, l_rs, t_ss, t_rs, r_ss, r_rs, d_ss, d_rs,
    e_ss, e_rs, s_ss, s_rs, a_ss, a_rs, p_ss, p_rs, x_ss, x_rs, f_ss, f_rs,
):
    seq, grp = lax.axis_index("seq"), lax.axis_index("grp")
    z, y = seq // NY, seq % NY
    x, core = grp // NC, grp % NC
    tokens, channels = x_ref.shape
    heads = channels // WIDTH
    pair = channels // NY
    cols = w_ref.shape[1]
    khalf = w_ref.shape[0] // 2
    thalf = tokens // 2

    def device(dz=0, dy=0, dx=0, dc=0):
        return (
            ((z + dz) % NZ) * NY + (y + dy) % NY,
            ((x + dx) % NX) * NC + (core + dc) % NC,
        )

    def remote(src, dst, ss, rs, to):
        return pltpu.make_async_remote_copy(
            src_ref=src, dst_ref=dst, send_sem=ss, recv_sem=rs, device_id=to, device_id_type=MESH
        )

    sends = []

    def send(src, dst, ss, rs, to):
        copy = remote(src, dst, ss, rs, to)
        copy.start()
        sends.append(copy)

    def arrived(dst, ss, rs):
        remote(dst, dst, ss, rs, device(dz=1)).wait_recv()

    barrier = pltpu.get_barrier_semaphore()
    others = (
        [dict(dz=k) for k in range(1, NZ)]
        + [dict(dy=k) for k in range(1, NY)]
        + [dict(dx=k) for k in range(1, NX)]
        + [dict(dc=1)]
    )
    for other in others:
        pl.semaphore_signal(barrier, inc=1, device_id=device(**other), device_id_type=MESH)

    raw = dt_ref[...] + bias_ref[...]
    dt = jnp.maximum(raw, 0.0) + jnp.log1p(jnp.exp(-jnp.abs(raw)))
    la = -jnp.exp(alog_ref[...]) * dt
    rows = lax.broadcasted_iota(jnp.int32, (tokens, tokens), 0)
    columns = lax.broadcasted_iota(jnp.int32, (tokens, tokens), 1)
    mask = rows >= columns
    cum = lax.dot_general(
        mask.astype(F32), la, (((1,), (0,)), ((), ())), precision=HIGH, preferred_element_type=F32
    )
    total = cum[tokens - 1 : tokens, :]
    weight = jnp.exp(total - cum) * dt

    pl.semaphore_wait(barrier, len(others))

    own_w = pltpu.make_async_copy(w_ref, wall.at[z], w_local)
    own_w.start()

    def w_part(origin, half):
        return wall.at[origin, pl.ds(half * khalf, khalf), :]

    for i in range(2):
        for d, sign in enumerate((1, -1)):
            half = i if d == 0 else 1 - i
            send(
                w_ref.at[pl.ds(half * khalf, khalf), :],
                w_part(z, half),
                w_ss.at[d, 0, i],
                w_rs.at[d, 0, i],
                device(dz=sign),
            )

    def relay(step, i):
        for d, sign in enumerate((1, -1)):
            half = i if d == 0 else 1 - i
            origin = (z - sign * step) % NZ
            arrived(w_part(origin, half), w_ss.at[d, step - 1, i], w_rs.at[d, step - 1, i])
            if step < NZ // 2 - 1 or (step == NZ // 2 - 1 and i == 0):
                send(
                    w_part(origin, half),
                    w_part(origin, half),
                    w_ss.at[d, step, i],
                    w_rs.at[d, step, i],
                    device(dz=sign),
                )

    bmat, cmat = b_ref[...], c_ref[...]
    for j in range(NY):
        parts = []
        for h in range(j * heads // NY, (j + 1) * heads // NY):
            xh = x_ref[:, h * WIDTH : (h + 1) * WIDTH].astype(F32)
            parts.append(xh * weight[:, h : h + 1])
        high, low = split(jnp.concatenate(parts, axis=1))
        state = dot(bmat, high, ((0,), (0,))) + dot(bmat, low, ((0,), (0,)))
        lsend[j] = state.astype(BF16)
        tsend[j] = jnp.concatenate(
            [
                jnp.broadcast_to(total[:, h : h + 1], (8, WIDTH))
                for h in range(j * heads // NY, (j + 1) * heads // NY)
            ],
            axis=1,
        )
    for k in range(1, NY):
        to = (y + k) % NY
        send(lsend.at[to], lrecv.at[y], l_ss.at[k - 1], l_rs.at[k - 1], device(dy=k))
        send(tsend.at[to], trecv.at[y], t_ss.at[k - 1], t_rs.at[k - 1], device(dy=k))
    lrecv[y] = lsend[y]
    trecv[y] = tsend[y]

    logits = dot(cmat, bmat, ((1,), (1,)))
    cum_t = jnp.transpose(cum)
    dt_t = jnp.transpose(dt)
    for h in range(heads):
        span = slice(h * WIDTH, (h + 1) * WIDTH)
        decay = jnp.exp(jnp.where(mask, cum[:, h : h + 1] - cum_t[h : h + 1, :], -1e30))
        high, low = split(decay * logits * dt_t[h : h + 1, :])
        xh = x_ref[:, span]
        ybuf[:, span] = dot(high, xh) + dot(low, xh) + skip_ref[:, h : h + 1] * xh.astype(F32)
        gate = m_ref[:, span].astype(F32)
        smbuf[:, span] = gate / (1.0 + jnp.exp(-gate))
    relay(1, 0)

    for k in range(1, NY):
        source = (y - k) % NY
        arrived(lrecv.at[source], l_ss.at[k - 1], l_rs.at[k - 1])
        arrived(trecv.at[source], t_ss.at[k - 1], t_rs.at[k - 1])
    before = [jnp.zeros((1, pair), F32)]
    current = lrecv[0].astype(F32)
    for j in range(NY):
        before.append(before[-1] + trecv[j][0:1, :])
        if j:
            current = jnp.exp(trecv[j][0:1, :]) * current + lrecv[j].astype(F32)
    size = STATE // NZ
    for k in range(NZ):
        rsend[k] = current[k * size : (k + 1) * size, :].astype(BF16)
    dsend[...] = jnp.broadcast_to(before[NY], (8, pair))
    for k in range(1, NZ):
        to = (z + k) % NZ
        send(rsend.at[to], rrecv.at[z], r_ss.at[k - 1], r_rs.at[k - 1], device(dz=k))
        send(dsend, drecv.at[z], d_ss.at[k - 1], d_rs.at[k - 1], device(dz=k))
    rrecv[z] = rsend[z]
    drecv[z] = dsend[...]
    current = lrecv[0].astype(F32)
    for j in range(1, NY):
        qbuf[j - 1] = current
        if j < NY - 1:
            current = jnp.exp(trecv[j][0:1, :]) * current + lrecv[j].astype(F32)
    relay(1, 1)

    for k in range(1, NZ):
        source = (z - k) % NZ
        arrived(rrecv.at[source], r_ss.at[k - 1], r_rs.at[k - 1])
        arrived(drecv.at[source], d_ss.at[k - 1], d_rs.at[k - 1])
    current = jnp.zeros((size, pair), F32)
    for k in range(NZ):
        esend[k] = current.astype(BF16)
        current = jnp.exp(drecv[k][0:1, :]) * current + rrecv[k].astype(F32)
    for k in range(1, NZ):
        to = (z + k) % NZ
        send(esend.at[to], erecv.at[z], e_ss.at[k - 1], e_rs.at[k - 1], device(dz=k))
    erecv[z] = esend[z]
    relay(2, 0)
    for k in range(1, NZ):
        source = (z - k) % NZ
        arrived(erecv.at[source], e_ss.at[k - 1], e_rs.at[k - 1])
    entry = jnp.concatenate([erecv[k].astype(F32) for k in range(NZ)], axis=0)
    ssend[0] = entry.astype(BF16)
    for j in range(1, NY):
        ssend[j] = (qbuf[j - 1] + jnp.exp(before[j]) * entry).astype(BF16)
    for k in range(1, NY):
        to = (y + k) % NY
        send(ssend.at[to], srecv.at[y], s_ss.at[k - 1], s_rs.at[k - 1], device(dy=k))
    srecv[y] = ssend[y]
    relay(2, 1)
    for k in range(1, NY):
        source = (y - k) % NY
        arrived(srecv.at[source], s_ss.at[k - 1], s_rs.at[k - 1])

    grown = jnp.exp(cum)
    squares = jnp.zeros((tokens, WIDTH), F32)
    for j in range(NY):
        inter = dot(cmat, srecv[j])
        for i in range(heads // NY):
            h = j * heads // NY + i
            span = slice(h * WIDTH, (h + 1) * WIDTH)
            value = ybuf[:, span] + grown[:, h : h + 1] * inter[:, i * WIDTH : (i + 1) * WIDTH]
            value = value * smbuf[:, span]
            ybuf[:, span] = value
            squares = squares + value * value
    mean = jnp.sum(squares, axis=1, keepdims=True) * (1.0 / channels)
    scale = lax.rsqrt(mean + 1e-05)
    abuf[y] = (ybuf[...] * scale * gain_ref[...]).astype(BF16)

    def a_part(origin, half):
        return abuf.at[origin, pl.ds(half * thalf, thalf), :]

    for i in range(2):
        for d, sign in enumerate((1, -1)):
            half = i if d == 0 else 1 - i
            part = a_part(y, half)
            send(part, part, a_ss.at[d, i], a_rs.at[d, i], device(dy=sign))
    relay(3, 0)
    for d, sign in enumerate((1, -1)):
        origin = (y - sign) % NY
        half = d
        part = a_part(origin, half)
        arrived(part, a_ss.at[d, 0], a_rs.at[d, 0])
        send(part, part, a_ss.at[d, 2], a_rs.at[d, 2], device(dy=sign))
    relay(3, 1)
    own_w.wait()
    relay(4, 0)

    turns = (0, -1, 1, 2)

    def multiply(t):
        if t == 0:
            pass
        elif t < 3:
            d = t - 1
            arrived(a_part((y + turns[t]) % NY, 1 - d), a_ss.at[d, 1], a_rs.at[d, 1])
        else:
            for d in range(2):
                arrived(a_part((y + 2) % NY, d), a_ss.at[d, 2], a_rs.at[d, 2])
        a = abuf[(y + turns[t]) % NY]
        for k in (2, 1, 3, 0):
            q = (x + k) % NX
            psend[t, k] = dot(a, wall[q * NC + 1 - core]).astype(BF16)
            send(psend.at[t, k], precv.at[t, k], p_ss.at[t, k], p_rs.at[t, k], device(dc=1))
            keep[t, k] = dot(a, wall[q * NC + core])

    def chip_sum(t):
        for k in (2, 1, 3, 0):
            arrived(precv.at[t, k], p_ss.at[t, k], p_rs.at[t, k])
            both = keep[t, k] + precv[t, k].astype(F32)
            if k:
                rssend[t, k - 1] = both.astype(BF16)
                send(
                    rssend.at[t, k - 1],
                    rsrecv.at[t, k - 1],
                    x_ss.at[t, k - 1],
                    x_rs.at[t, k - 1],
                    device(dx=k),
                )
            else:
                keep[t, k] = both

    mine = pl.ds(pl.multiple_of(y * cols, cols), cols)

    def finish(t):
        value = keep[t, 0]
        for k in range(1, NX):
            arrived(rsrecv.at[t, k - 1], x_ss.at[t, k - 1], x_rs.at[t, k - 1])
            value = value + rsrecv[t, k - 1].astype(F32)
        if t == 0:
            out_ref[:, mine] = value.astype(BF16)
        else:
            fsend[t - 1] = value.astype(BF16)
            send(
                fsend.at[t - 1],
                out_ref.at[:, mine],
                f_ss.at[t - 1],
                f_rs.at[t - 1],
                device(dy=turns[t]),
            )

    for t in range(NY + 2):
        if t < NY:
            multiply(t)
        if 1 <= t <= NY:
            chip_sum(t - 1)
        if t >= 2:
            finish(t - 2)
    for t in range(1, NY):
        source = (y - turns[t]) % NY
        span = pl.ds(pl.multiple_of(source * cols, cols), cols)
        arrived(out_ref.at[:, span], f_ss.at[t - 1], f_rs.at[t - 1])
    for copy in sends:
        copy.wait_send()


def shards(
    x_in, multiplier_channels, b_proj, c_proj, dt_raw, dt_bias, a_log, skip_d, norm_gain, w_out
):
    tokens, channels = x_in.shape
    depth, cols = w_out.shape
    pair = channels // NY
    size = STATE // NZ
    vmem = pl.BlockSpec(memory_space=pltpu.VMEM)
    dma = pltpu.SemaphoreType.DMA
    scratch = [
        pltpu.VMEM((NZ, depth, cols), BF16),
        pltpu.VMEM((NY, tokens, channels), BF16),
        pltpu.VMEM((tokens, channels), F32),
        pltpu.VMEM((tokens, channels), F32),
        pltpu.VMEM((NY - 1, STATE, pair), F32),
        pltpu.VMEM((NY, STATE, pair), BF16),
        pltpu.VMEM((NY, STATE, pair), BF16),
        pltpu.VMEM((NY, 8, pair), F32),
        pltpu.VMEM((NY, 8, pair), F32),
        pltpu.VMEM((NZ, size, pair), BF16),
        pltpu.VMEM((NZ, size, pair), BF16),
        pltpu.VMEM((8, pair), F32),
        pltpu.VMEM((NZ, 8, pair), F32),
        pltpu.VMEM((NZ, size, pair), BF16),
        pltpu.VMEM((NZ, size, pair), BF16),
        pltpu.VMEM((NY, STATE, pair), BF16),
        pltpu.VMEM((NY, STATE, pair), BF16),
        pltpu.VMEM((NY, NX, tokens, cols), BF16),
        pltpu.VMEM((NY, NX, tokens, cols), BF16),
        pltpu.VMEM((NY, NX, tokens, cols), F32),
        pltpu.VMEM((NY, NX - 1, tokens, cols), BF16),
        pltpu.VMEM((NY, NX - 1, tokens, cols), BF16),
        pltpu.VMEM((NY - 1, tokens, cols), BF16),
        dma,
        dma((2, 4, 2)), dma((2, 4, 2)),
        dma((3,)), dma((3,)), dma((3,)), dma((3,)),
        dma((7,)), dma((7,)), dma((7,)), dma((7,)),
        dma((7,)), dma((7,)),
        dma((3,)), dma((3,)),
        dma((2, 3)), dma((2, 3)),
        dma((4, 4)), dma((4, 4)),
        dma((4, 3)), dma((4, 3)),
        dma((3,)), dma((3,)),
    ]
    return pl.pallas_call(
        kernel,
        out_shape=jax.ShapeDtypeStruct((tokens, channels), BF16),
        in_specs=[vmem] * 9 + [pl.BlockSpec(memory_space=pl.ANY)],
        out_specs=vmem,
        scratch_shapes=scratch,
        compiler_params=pltpu.CompilerParams(
            collective_id=0, has_side_effects=True, vmem_limit_bytes=56 * 1024 * 1024
        ),
        name="mixer",
    )(
        x_in,
        multiplier_channels,
        b_proj,
        c_proj,
        dt_raw,
        dt_bias.reshape(1, -1),
        a_log.reshape(1, -1),
        skip_d.reshape(1, -1),
        norm_gain.reshape(1, -1),
        w_out,
    )


def solution(mesh):
    return jax.shard_map(
        shards,
        mesh=mesh,
        in_specs=(
            P("seq", "grp"),
            P("seq", "grp"),
            P("seq", "grp"),
            P("seq", "grp"),
            P("seq", "grp"),
            P("grp"),
            P("grp"),
            P("grp"),
            P("grp"),
            P("grp", "seq"),
        ),
        out_specs=P("seq", "grp"),
        check_vma=False,
    )
```

```python
import jax
import jax.numpy as jnp
from jax import lax
from jax.experimental import pallas as pl
from jax.experimental.pallas import tpu as pltpu
from jax.sharding import PartitionSpec as P

MESH = pl.DeviceIdType.MESH
HIGH = lax.Precision.HIGHEST
WIDTH = 128
STATE = 128
NZ, NY, NX, NC = 8, 4, 4, 2
F32 = jnp.float32
BF16 = jnp.bfloat16


def split(value):
    high = value.astype(BF16)
    return high, (value - high.astype(F32)).astype(BF16)


def dot(a, b, dims=((1,), (0,))):
    return lax.dot_general(a, b, (dims, ((), ())), preferred_element_type=F32)


def kernel(
    dt_ref, bias_ref, alog_ref, skip_ref, gain_ref, b_ref, c_ref, x_ref, m_ref, w_ref,
    out_ref,
    wall, abuf, ybuf, smbuf, qbuf,
    lsend, lrecv, tsend, trecv,
    rsend, rrecv, dsend, drecv,
    esend, erecv, ssend, srecv,
    pgive, precv, pkeep, xsend, xrecv, fsend,
    w_local, w_ss, w_rs, l_ss, l_rs, t_ss, t_rs, r_ss, r_rs, d_ss, d_rs,
    e_ss, e_rs, s_ss, s_rs, a_ss, a_rs, p_ss, p_rs, x_ss, x_rs, f_ss, f_rs,
):
    seq, grp = lax.axis_index("seq"), lax.axis_index("grp")
    z, y = seq // NY, seq % NY
    x, core = grp // NC, grp % NC
    tokens, channels = x_ref.shape
    heads = channels // WIDTH
    pair = channels // NY
    cols = w_ref.shape[1]
    khalf = w_ref.shape[0] // 2
    chalf = cols // 2
    thalf = tokens // 2
    share = NY * tokens // NC

    def device(dz=0, dy=0, dx=0, dc=0):
        return (
            ((z + dz) % NZ) * NY + (y + dy) % NY,
            ((x + dx) % NX) * NC + (core + dc) % NC,
        )

    def remote(src, dst, ss, rs, to):
        return pltpu.make_async_remote_copy(
            src_ref=src, dst_ref=dst, send_sem=ss, recv_sem=rs, device_id=to, device_id_type=MESH
        )

    sends = []

    def send(src, dst, ss, rs, to):
        copy = remote(src, dst, ss, rs, to)
        copy.start()
        sends.append(copy)

    def arrived(dst, ss, rs):
        remote(dst, dst, ss, rs, device(dz=1)).wait_recv()

    barrier = pltpu.get_barrier_semaphore()
    others = (
        [dict(dz=k) for k in range(1, NZ)]
        + [dict(dy=k) for k in range(1, NY)]
        + [dict(dx=k, dc=c) for k in range(NX) for c in range(NC) if k or c]
    )
    for other in others:
        pl.semaphore_signal(barrier, inc=1, device_id=device(**other), device_id_type=MESH)
    own_w = []
    for i in range(2):
        copy = pltpu.make_async_copy(
            w_ref.at[:, i * chalf : (i + 1) * chalf], wall.at[z, i], w_local.at[i]
        )
        copy.start()
        own_w.append(copy)

    raw = jnp.transpose(dt_ref[...]) + bias_ref[...]
    dt = jnp.maximum(raw, 0.0) + jnp.log1p(jnp.exp(-jnp.abs(raw)))
    la = -jnp.exp(alog_ref[...]) * dt
    rows = lax.broadcasted_iota(jnp.int32, (tokens, tokens), 0)
    columns = lax.broadcasted_iota(jnp.int32, (tokens, tokens), 1)
    mask = rows >= columns
    cum = lax.dot_general(
        mask.astype(F32), la, (((1,), (0,)), ((), ())), precision=HIGH, preferred_element_type=F32
    )
    total = cum[tokens - 1 : tokens, :]
    weight = jnp.exp(total - cum) * dt

    for copy in own_w:
        copy.wait()
    pl.semaphore_wait(barrier, len(others))

    def w_part(origin, d, i):
        half = i % 2 if d == 0 else 1 - i % 2
        return wall.at[origin, i // 2, pl.ds(half * khalf, khalf), :]

    for i in range(4):
        for d, sign in enumerate((1, -1)):
            part = w_part(z, d, i)
            send(part, part, w_ss.at[d, 0, i], w_rs.at[d, 0, i], device(dz=sign))

    last = NZ // 2
    items = [(step, i) for step in range(1, last) for i in range(4)] + [(last, 0), (last, 2)]
    done = [0]

    def relay(count):
        while done[0] < count:
            step, i = items[done[0]]
            done[0] += 1
            for d, sign in enumerate((1, -1)):
                part = w_part((z - sign * step) % NZ, d, i)
                arrived(part, w_ss.at[d, step - 1, i], w_rs.at[d, step - 1, i])
                if step < last - 1 or (step == last - 1 and i % 2 == 0):
                    send(part, part, w_ss.at[d, step, i], w_rs.at[d, step, i], device(dz=sign))

    bmat, cmat = b_ref[...], c_ref[...]
    for j in range(NY):
        parts = []
        for h in range(j * heads // NY, (j + 1) * heads // NY):
            xh = x_ref[:, h * WIDTH : (h + 1) * WIDTH].astype(F32)
            parts.append(xh * weight[:, h : h + 1])
        high, low = split(jnp.concatenate(parts, axis=1))
        state = dot(bmat, high, ((0,), (0,))) + dot(bmat, low, ((0,), (0,)))
        lsend[j] = state.astype(BF16)
        tsend[j] = jnp.concatenate(
            [
                jnp.broadcast_to(total[:, h : h + 1], (8, WIDTH))
                for h in range(j * heads // NY, (j + 1) * heads // NY)
            ],
            axis=1,
        )
    for k in range(1, NY):
        to = (y + k) % NY
        send(lsend.at[to], lrecv.at[y], l_ss.at[k - 1], l_rs.at[k - 1], device(dy=k))
        send(tsend.at[to], trecv.at[y], t_ss.at[k - 1], t_rs.at[k - 1], device(dy=k))
    lrecv[y] = lsend[y]
    trecv[y] = tsend[y]

    logits = dot(cmat, bmat, ((1,), (1,)))
    cum_t = jnp.transpose(cum)
    dt_t = jnp.transpose(dt)
    for h in range(heads):
        span = slice(h * WIDTH, (h + 1) * WIDTH)
        decay = jnp.exp(jnp.where(mask, cum[:, h : h + 1] - cum_t[h : h + 1, :], -1e30))
        high, low = split(decay * logits * dt_t[h : h + 1, :])
        xh = x_ref[:, span]
        ybuf[:, span] = dot(high, xh) + dot(low, xh) + skip_ref[:, h : h + 1] * xh.astype(F32)
        gate = m_ref[:, span].astype(F32)
        smbuf[:, span] = gate / (1.0 + jnp.exp(-gate))

    for k in range(1, NY):
        source = (y - k) % NY
        arrived(lrecv.at[source], l_ss.at[k - 1], l_rs.at[k - 1])
        arrived(trecv.at[source], t_ss.at[k - 1], t_rs.at[k - 1])
    before = [jnp.zeros((1, pair), F32)]
    current = lrecv[0].astype(F32)
    for j in range(NY):
        before.append(before[-1] + trecv[j][0:1, :])
        if j:
            qbuf[j - 1] = current
            current = jnp.exp(trecv[j][0:1, :]) * current + lrecv[j].astype(F32)
    size = STATE // NZ
    for k in range(NZ):
        rsend[k] = current[k * size : (k + 1) * size, :]
    dsend[...] = jnp.broadcast_to(before[NY], (8, pair))
    for k in range(1, NZ):
        to = (z + k) % NZ
        send(rsend.at[to], rrecv.at[z], r_ss.at[k - 1], r_rs.at[k - 1], device(dz=k))
        send(dsend, drecv.at[z], d_ss.at[k - 1], d_rs.at[k - 1], device(dz=k))
    rrecv[z] = rsend[z]
    drecv[z] = dsend[...]
    relay(2)

    for k in range(1, NZ):
        source = (z - k) % NZ
        arrived(rrecv.at[source], r_ss.at[k - 1], r_rs.at[k - 1])
        arrived(drecv.at[source], d_ss.at[k - 1], d_rs.at[k - 1])
    current = jnp.zeros((size, pair), F32)
    for k in range(NZ):
        esend[k] = current
        current = jnp.exp(drecv[k][0:1, :]) * current + rrecv[k]
    for k in range(1, NZ):
        to = (z + k) % NZ
        send(esend.at[to], erecv.at[z], e_ss.at[k - 1], e_rs.at[k - 1], device(dz=k))
    erecv[z] = esend[z]
    relay(4)
    for k in range(1, NZ):
        source = (z - k) % NZ
        arrived(erecv.at[source], e_ss.at[k - 1], e_rs.at[k - 1])
    entry = jnp.concatenate([erecv[k] for k in range(NZ)], axis=0)
    ssend[0] = entry.astype(BF16)
    for j in range(1, NY):
        ssend[j] = (qbuf[j - 1] + jnp.exp(before[j]) * entry).astype(BF16)
    for k in range(1, NY):
        to = (y + k) % NY
        send(ssend.at[to], srecv.at[y], s_ss.at[k - 1], s_rs.at[k - 1], device(dy=k))
    srecv[y] = ssend[y]
    relay(6)
    for k in range(1, NY):
        source = (y - k) % NY
        arrived(srecv.at[source], s_ss.at[k - 1], s_rs.at[k - 1])

    grown = jnp.exp(cum)
    squares = jnp.zeros((tokens, WIDTH), F32)
    for j in range(NY):
        inter = dot(cmat, srecv[j])
        for i in range(heads // NY):
            h = j * heads // NY + i
            span = slice(h * WIDTH, (h + 1) * WIDTH)
            value = ybuf[:, span] + grown[:, h : h + 1] * inter[:, i * WIDTH : (i + 1) * WIDTH]
            value = value * smbuf[:, span]
            ybuf[:, span] = value
            squares = squares + value * value
    mean = jnp.sum(squares, axis=1, keepdims=True) * (1.0 / channels)
    scale = lax.rsqrt(mean + 1e-05)
    abuf[y] = (ybuf[...] * scale * gain_ref[...]).astype(BF16)

    def a_part(origin, half):
        return abuf.at[origin, pl.ds(half * thalf, thalf), :]

    for i in range(2):
        for d, sign in enumerate((1, -1)):
            part = a_part(y, i if d == 0 else 1 - i)
            send(part, part, a_ss.at[d, i], a_rs.at[d, i], device(dy=sign))
    relay(8)
    for d, sign in enumerate((1, -1)):
        part = a_part((y - sign) % NY, d)
        arrived(part, a_ss.at[d, 0], a_rs.at[d, 0])
        send(part, part, a_ss.at[d, 2], a_rs.at[d, 2], device(dy=sign))
    relay(10)
    for d, sign in enumerate((1, -1)):
        arrived(a_part((y - sign) % NY, 1 - d), a_ss.at[d, 1], a_rs.at[d, 1])
    for d in range(2):
        arrived(a_part((y + 2) % NY, d), a_ss.at[d, 2], a_rs.at[d, 2])

    distances = (0, 1, -1, 2, -2, 3, -3, 4)

    def rows_of(which):
        first = pl.multiple_of(which * (NY // NC), NY // NC)
        return abuf[pl.ds(first, NY // NC)].reshape(share, channels)

    def multiply(n, halves):
        origin = (z + distances[n]) % NZ
        part = jnp.concatenate([wall[origin, i] for i in halves], axis=1)
        give = dot(rows_of(1 - core), part)
        for i in halves:
            first = (i - halves[0]) * chalf
            pgive[n, i] = give[:, first : first + chalf]
            send(pgive.at[n, i], precv.at[n, i], p_ss.at[n, i], p_rs.at[n, i], device(dc=1))
        held = dot(rows_of(core), part)
        for i in halves:
            first = (i - halves[0]) * chalf
            pkeep[n, i] = held[:, first : first + chalf]

    mine = pl.ds(pl.multiple_of(core * share, share), share)

    def owner(n):
        origin = (z + distances[n]) % NZ
        return origin // NC, origin % NC

    def chip_sum(n, halves):
        to_x, to_core = owner(n)
        own = (to_x == x) & (to_core == core)
        for i in halves:
            arrived(precv.at[n, i], p_ss.at[n, i], p_rs.at[n, i])
            both = (pkeep[n, i] + precv[n, i]).astype(BF16)
            xsend[n, i] = both

            @pl.when(own)
            def _():
                xrecv[x, i, mine, :] = xsend[n, i]

            @pl.when(jnp.logical_not(own))
            def _():
                remote(
                    xsend.at[n, i],
                    xrecv.at[x, i, mine, :],
                    x_ss.at[n, i],
                    x_rs.at[x, core, i],
                    (seq, to_x * NC + to_core),
                ).start()

    units = [(n, (0, 1)) for n in range(NZ - 1)] + [(NZ - 1, (0,)), (NZ - 1, (1,))]
    needed = [0, 4, 4, 8, 8, 12, 12, 13, 14]
    for u, (n, halves) in enumerate(units):
        relay(needed[u])
        multiply(n, halves)
        if u:
            chip_sum(*units[u - 1])
    chip_sum(*units[-1])

    for i in range(2):
        for k in range(NX):
            for c in range(NC):
                if k or c:
                    from_x, from_core = (x + k) % NX, (core + c) % NC
                    spot = pl.ds(pl.multiple_of(from_core * share, share), share)
                    arrived(
                        xrecv.at[from_x, i, spot, :], x_ss.at[0, i], x_rs.at[from_x, from_core, i]
                    )
        lanes = pl.ds(pl.multiple_of(y * cols + i * chalf, chalf), chalf)
        for k in (2, 1, 3, 0):
            to = (y + k) % NY
            spot = pl.ds(pl.multiple_of(to * tokens, tokens), tokens)
            value = xrecv[0, i, spot, :].astype(F32)
            for j in range(1, NX):
                value = value + xrecv[j, i, spot, :].astype(F32)
            if k:
                fsend[k - 1, i] = value.astype(BF16)
                send(
                    fsend.at[k - 1, i],
                    out_ref.at[:, lanes],
                    f_ss.at[k - 1, i],
                    f_rs.at[k - 1, i],
                    device(dy=k),
                )
            else:
                out_ref[:, lanes] = value.astype(BF16)
    for i in range(2):
        for k in range(1, NY):
            source = (y - k) % NY
            lanes = pl.ds(pl.multiple_of(source * cols + i * chalf, chalf), chalf)
            arrived(out_ref.at[:, lanes], f_ss.at[k - 1, i], f_rs.at[k - 1, i])
    for copy in sends:
        copy.wait_send()
    for n in range(NZ):
        to_x, to_core = owner(n)

        @pl.when((to_x != x) | (to_core != core))
        def _():
            for i in range(2):
                remote(
                    xsend.at[n, i],
                    xrecv.at[x, i, mine, :],
                    x_ss.at[n, i],
                    x_rs.at[x, core, i],
                    (seq, to_x * NC + to_core),
                ).wait_send()


def shards(
    x_in, multiplier_channels, b_proj, c_proj, dt_raw, dt_bias, a_log, skip_d, norm_gain, w_out
):
    tokens, channels = x_in.shape
    depth, cols = w_out.shape
    pair = channels // NY
    size = STATE // NZ
    vmem = pl.BlockSpec(memory_space=pltpu.VMEM)
    dma = pltpu.SemaphoreType.DMA
    half = cols // 2
    share = NY * tokens // NC
    scratch = [
        pltpu.VMEM((NZ, 2, depth, half), BF16),
        pltpu.VMEM((NY, tokens, channels), BF16),
        pltpu.VMEM((tokens, channels), F32),
        pltpu.VMEM((tokens, channels), F32),
        pltpu.VMEM((NY - 1, STATE, pair), F32),
        pltpu.VMEM((NY, STATE, pair), BF16),
        pltpu.VMEM((NY, STATE, pair), BF16),
        pltpu.VMEM((NY, 8, pair), F32),
        pltpu.VMEM((NY, 8, pair), F32),
        pltpu.VMEM((NZ, size, pair), F32),
        pltpu.VMEM((NZ, size, pair), F32),
        pltpu.VMEM((8, pair), F32),
        pltpu.VMEM((NZ, 8, pair), F32),
        pltpu.VMEM((NZ, size, pair), F32),
        pltpu.VMEM((NZ, size, pair), F32),
        pltpu.VMEM((NY, STATE, pair), BF16),
        pltpu.VMEM((NY, STATE, pair), BF16),
        pltpu.VMEM((NZ, 2, share, half), F32),
        pltpu.VMEM((NZ, 2, share, half), F32),
        pltpu.VMEM((NZ, 2, share, half), F32),
        pltpu.VMEM((NZ, 2, share, half), BF16),
        pltpu.VMEM((NX, 2, NY * tokens, half), BF16),
        pltpu.VMEM((NY - 1, 2, tokens, half), BF16),
        dma((2,)),
        dma((2, 4, 4)), dma((2, 4, 4)),
        dma((3,)), dma((3,)), dma((3,)), dma((3,)),
        dma((7,)), dma((7,)), dma((7,)), dma((7,)),
        dma((7,)), dma((7,)),
        dma((3,)), dma((3,)),
        dma((2, 3)), dma((2, 3)),
        dma((NZ, 2)), dma((NZ, 2)),
        dma((NZ, 2)), dma((NX, NC, 2)),
        dma((NY - 1, 2)), dma((NY - 1, 2)),
    ]
    return pl.pallas_call(
        kernel,
        out_shape=jax.ShapeDtypeStruct((tokens, channels), BF16),
        in_specs=[vmem] * 9 + [pl.BlockSpec(memory_space=pl.ANY)],
        out_specs=vmem,
        scratch_shapes=scratch,
        compiler_params=pltpu.CompilerParams(
            collective_id=0, has_side_effects=True, vmem_limit_bytes=56 * 1024 * 1024
        ),
        name="mixer",
    )(
        dt_raw.T,
        dt_bias.reshape(1, -1),
        a_log.reshape(1, -1),
        skip_d.reshape(1, -1),
        norm_gain.reshape(1, -1),
        b_proj,
        c_proj,
        x_in,
        multiplier_channels,
        w_out,
    )


def solution(mesh):
    return jax.shard_map(
        shards,
        mesh=mesh,
        in_specs=(
            P("seq", "grp"),
            P("seq", "grp"),
            P("seq", "grp"),
            P("seq", "grp"),
            P("seq", "grp"),
            P("grp"),
            P("grp"),
            P("grp"),
            P("grp"),
            P("grp", "seq"),
        ),
        out_specs=P("seq", "grp"),
        check_vma=False,
    )
```

```python
import jax
import jax.numpy as jnp
from jax import lax
from jax.experimental import pallas as pl
from jax.experimental.pallas import tpu as pltpu
from jax.sharding import PartitionSpec as P

MESH = pl.DeviceIdType.MESH
HIGH = lax.Precision.HIGHEST
WIDTH = 128
STATE = 128
NZ, NY, NX, NC = 8, 4, 4, 2
F32 = jnp.float32
BF16 = jnp.bfloat16


def split(value):
    high = value.astype(BF16)
    return high, (value - high.astype(F32)).astype(BF16)


def dot(a, b, dims=((1,), (0,))):
    return lax.dot_general(a, b, (dims, ((), ())), preferred_element_type=F32)


def kernel(
    dt_ref, bias_ref, alog_ref, skip_ref, gain_ref, b_ref, c_ref, x_ref, m_ref, w_ref,
    out_ref,
    wall, abuf, ybuf, smbuf, qbuf,
    lsend, lrecv, tsend, trecv,
    rsend, rrecv, dsend, drecv,
    esend, erecv, ssend, srecv,
    part_sums, precv, xsend, xrecv, fsend,
    w_local, w_ss, w_rs, l_ss, l_rs, t_ss, t_rs, r_ss, r_rs, d_ss, d_rs,
    e_ss, e_rs, s_ss, s_rs, a_ss, a_rs, p_ss, p_rs, x_ss, x_rs, f_ss, f_rs,
):
    seq, grp = lax.axis_index("seq"), lax.axis_index("grp")
    z, y = seq // NY, seq % NY
    x, core = grp // NC, grp % NC
    tokens, channels = x_ref.shape
    heads = channels // WIDTH
    pair = channels // NY
    cols = w_ref.shape[1]
    khalf = w_ref.shape[0] // 2
    chalf = cols // 2
    thalf = tokens // 2
    share = tokens // NC

    def device(dz=0, dy=0, dx=0, dc=0):
        return (
            ((z + dz) % NZ) * NY + (y + dy) % NY,
            ((x + dx) % NX) * NC + (core + dc) % NC,
        )

    def remote(src, dst, ss, rs, to):
        return pltpu.make_async_remote_copy(
            src_ref=src, dst_ref=dst, send_sem=ss, recv_sem=rs, device_id=to, device_id_type=MESH
        )

    sends = []

    def send(src, dst, ss, rs, to):
        copy = remote(src, dst, ss, rs, to)
        copy.start()
        sends.append(copy)

    def arrived(dst, ss, rs):
        remote(dst, dst, ss, rs, device(dz=1)).wait_recv()

    barrier = pltpu.get_barrier_semaphore()
    others = (
        [dict(dz=k) for k in range(1, NZ)]
        + [dict(dy=k) for k in range(1, NY)]
        + [dict(dx=k, dc=c) for k in range(NX) for c in range(NC) if k or c]
    )
    for other in others:
        pl.semaphore_signal(barrier, inc=1, device_id=device(**other), device_id_type=MESH)
    own_w = []
    for i in range(2):
        copy = pltpu.make_async_copy(
            w_ref.at[:, i * chalf : (i + 1) * chalf], wall.at[z, i], w_local.at[i]
        )
        copy.start()
        own_w.append(copy)

    raw = jnp.transpose(dt_ref[...]) + bias_ref[...]
    dt = jnp.maximum(raw, 0.0) + jnp.log1p(jnp.exp(-jnp.abs(raw)))
    la = -jnp.exp(alog_ref[...]) * dt
    rows = lax.broadcasted_iota(jnp.int32, (tokens, tokens), 0)
    columns = lax.broadcasted_iota(jnp.int32, (tokens, tokens), 1)
    mask = rows >= columns
    cum = lax.dot_general(
        mask.astype(F32), la, (((1,), (0,)), ((), ())), precision=HIGH, preferred_element_type=F32
    )
    total = cum[tokens - 1 : tokens, :]
    weight = jnp.exp(total - cum) * dt

    bmat, cmat = b_ref[...], c_ref[...]
    for j in range(NY):
        parts = []
        for h in range(j * heads // NY, (j + 1) * heads // NY):
            xh = x_ref[:, h * WIDTH : (h + 1) * WIDTH].astype(F32)
            parts.append(xh * weight[:, h : h + 1])
        high, low = split(jnp.concatenate(parts, axis=1))
        state = dot(bmat, high, ((0,), (0,))) + dot(bmat, low, ((0,), (0,)))
        lsend[j] = state.astype(BF16)
        tsend[j] = jnp.concatenate(
            [
                jnp.broadcast_to(total[:, h : h + 1], (8, WIDTH))
                for h in range(j * heads // NY, (j + 1) * heads // NY)
            ],
            axis=1,
        )
    logits = dot(cmat, bmat, ((1,), (1,)))
    cum_t = jnp.transpose(cum)
    dt_t = jnp.transpose(dt)
    for h in range(heads):
        span = slice(h * WIDTH, (h + 1) * WIDTH)
        decay = jnp.exp(jnp.where(mask, cum[:, h : h + 1] - cum_t[h : h + 1, :], -1e30))
        high, low = split(decay * logits * dt_t[h : h + 1, :])
        xh = x_ref[:, span]
        ybuf[:, span] = dot(high, xh) + dot(low, xh) + skip_ref[:, h : h + 1] * xh.astype(F32)
        gate = m_ref[:, span].astype(F32)
        smbuf[:, span] = gate / (1.0 + jnp.exp(-gate))

    for copy in own_w:
        copy.wait()
    pl.semaphore_wait(barrier, len(others))

    for k in range(1, NY):
        to = (y + k) % NY
        send(lsend.at[to], lrecv.at[y], l_ss.at[k - 1], l_rs.at[k - 1], device(dy=k))
        send(tsend.at[to, pl.ds(0, 1), :], trecv.at[y, pl.ds(0, 1), :], t_ss.at[k - 1], t_rs.at[k - 1], device(dy=k))
    lrecv[y] = lsend[y]
    trecv[y] = tsend[y]

    def w_part(origin, d, i):
        half = i % 2 if d == 0 else 1 - i % 2
        return wall.at[origin, i // 2, pl.ds(half * khalf, khalf), :]

    last = NZ // 2
    items = [(step, i) for step in range(last) for i in range(4)] + [(last, 0), (last, 2)]
    done = [0]

    def relay(count):
        while done[0] < count:
            step, i = items[done[0]]
            done[0] += 1
            for d, sign in enumerate((1, -1)):
                part = w_part((z - sign * step) % NZ, d, i)
                if step:
                    arrived(part, w_ss.at[d, step - 1, i], w_rs.at[d, step - 1, i])
                if step < last - 1 or (step == last - 1 and i % 2 == 0):
                    send(part, part, w_ss.at[d, step, i], w_rs.at[d, step, i], device(dz=sign))

    relay(2)

    for k in range(1, NY):
        source = (y - k) % NY
        arrived(lrecv.at[source], l_ss.at[k - 1], l_rs.at[k - 1])
        arrived(trecv.at[source, pl.ds(0, 1), :], t_ss.at[k - 1], t_rs.at[k - 1])
    before = [jnp.zeros((1, pair), F32)]
    current = lrecv[0].astype(F32)
    for j in range(NY):
        before.append(before[-1] + trecv[j][0:1, :])
        if j:
            qbuf[j - 1] = current
            current = jnp.exp(trecv[j][0:1, :]) * current + lrecv[j].astype(F32)
    size = STATE // NZ
    for k in range(NZ):
        rsend[k] = current[k * size : (k + 1) * size, :].astype(BF16)
    dsend[...] = jnp.broadcast_to(before[NY], (8, pair))
    for k in range(1, NZ):
        to = (z + k) % NZ
        send(rsend.at[to], rrecv.at[z], r_ss.at[k - 1], r_rs.at[k - 1], device(dz=k))
        send(dsend.at[pl.ds(0, 1), :], drecv.at[z, pl.ds(0, 1), :], d_ss.at[k - 1], d_rs.at[k - 1], device(dz=k))
    rrecv[z] = rsend[z]
    drecv[z] = dsend[...]
    relay(5)

    for k in range(1, NZ):
        source = (z - k) % NZ
        arrived(rrecv.at[source], r_ss.at[k - 1], r_rs.at[k - 1])
        arrived(drecv.at[source, pl.ds(0, 1), :], d_ss.at[k - 1], d_rs.at[k - 1])
    current = jnp.zeros((size, pair), F32)
    for k in range(NZ):
        esend[k] = current.astype(BF16)
        current = jnp.exp(drecv[k][0:1, :]) * current + rrecv[k].astype(F32)
    for k in range(1, NZ):
        to = (z + k) % NZ
        send(esend.at[to], erecv.at[z], e_ss.at[k - 1], e_rs.at[k - 1], device(dz=k))
    erecv[z] = esend[z]
    relay(8)
    for k in range(1, NZ):
        source = (z - k) % NZ
        arrived(erecv.at[source], e_ss.at[k - 1], e_rs.at[k - 1])
    entry = jnp.concatenate([erecv[k].astype(F32) for k in range(NZ)], axis=0)
    ssend[0] = entry.astype(BF16)
    for j in range(1, NY):
        ssend[j] = (qbuf[j - 1] + jnp.exp(before[j]) * entry).astype(BF16)
    for k in range(1, NY):
        to = (y + k) % NY
        send(ssend.at[to], srecv.at[y], s_ss.at[k - 1], s_rs.at[k - 1], device(dy=k))
    srecv[y] = ssend[y]
    relay(10)
    for k in range(1, NY):
        source = (y - k) % NY
        arrived(srecv.at[source], s_ss.at[k - 1], s_rs.at[k - 1])

    grown = jnp.exp(cum)
    squares = jnp.zeros((tokens, WIDTH), F32)
    for j in range(NY):
        inter = dot(cmat, srecv[j])
        for i in range(heads // NY):
            h = j * heads // NY + i
            span = slice(h * WIDTH, (h + 1) * WIDTH)
            value = ybuf[:, span] + grown[:, h : h + 1] * inter[:, i * WIDTH : (i + 1) * WIDTH]
            value = value * smbuf[:, span]
            ybuf[:, span] = value
            squares = squares + value * value
    mean = jnp.sum(squares, axis=1, keepdims=True) * (1.0 / channels)
    scale = lax.rsqrt(mean + 1e-05)
    abuf[0] = (ybuf[...] * scale * gain_ref[...]).astype(BF16)

    turns = (0, -1, 1, 2)

    def a_part(turn, half):
        return abuf.at[turn, pl.ds(half * thalf, thalf), :]

    for i in range(2):
        for d, sign in enumerate((1, -1)):
            half = i if d == 0 else 1 - i
            send(
                a_part(0, half),
                a_part(1 + d, half),
                a_ss.at[d, i],
                a_rs.at[d, i],
                device(dy=sign),
            )

    distances = (0, 1, -1, 2, -2, 3, -3, 4)
    stages = ((0, 1), (1, 3), (3, 4))
    whole = (0, NY)

    def owner(n):
        origin = (z + distances[n]) % NZ
        return origin // NC, origin % NC

    def partner_copy(n, span):
        rows = pl.ds(span[0], span[1] - span[0])
        index = 0 if span == whole else stages.index(span)
        return (
            part_sums.at[1 - core, n, rows],
            precv.at[n, rows],
            p_ss.at[n, index],
            p_rs.at[n, index],
        )

    def multiply(n, span):
        count = span[1] - span[0]
        origin = (z + distances[n]) % NZ
        part = jnp.concatenate([wall[origin, 0], wall[origin, 1]], axis=1)
        if span == whole:
            for first in (0, 2):
                a = abuf[first : first + 2].reshape(2 * tokens, channels)
                total = dot(a, part).reshape(2, tokens, cols)
                for c in range(NC):
                    part_sums[c, n, first : first + 2] = total[:, c * share : (c + 1) * share, :]
        else:
            a = abuf[span[0] : span[1]].reshape(count * tokens, channels)
            total = dot(a, part).reshape(count, tokens, cols)
            for c in range(NC):
                part_sums[c, n, span[0] : span[1]] = total[:, c * share : (c + 1) * share, :]
        send(*partner_copy(n, span), device(dc=1))

    def owner_copy(n, index):
        rows = pl.ds(stages[index][0], stages[index][1] - stages[index][0])
        to_x, to_core = owner(n)
        return remote(
            xsend.at[n, rows],
            xrecv.at[x, core, rows],
            x_ss.at[n, index],
            x_rs.at[x, core, index],
            (seq, to_x * NC + to_core),
        )

    def chip_sum(n, span):
        to_x, to_core = owner(n)
        own = (to_x == x) & (to_core == core)
        _, dst, ss, rs = partner_copy(n, span)
        arrived(dst, ss, rs)
        rows = slice(*span)
        both = part_sums[core, n, rows] + precv[n, rows]
        xsend[n, rows] = both.astype(BF16)

        @pl.when(own)
        def _():
            xrecv[x, core, rows] = xsend[n, rows]

        @pl.when(jnp.logical_not(own))
        def _():
            for index in range(3) if span == whole else (stages.index(span),):
                owner_copy(n, index).start()

    pending = []

    def unit(n, span):
        multiply(n, span)
        pending.append((n, span))
        if len(pending) > 1:
            chip_sum(*pending.pop(0))

    relay(11)
    for n in range(3):
        unit(n, stages[0])
    relay(12)
    for d, sign in enumerate((1, -1)):
        arrived(a_part(1 + d, d), a_ss.at[d, 0], a_rs.at[d, 0])
        send(a_part(1 + d, d), a_part(3, d), a_ss.at[d, 2], a_rs.at[d, 2], device(dy=sign))
    relay(13)
    for n in range(3, 5):
        unit(n, stages[0])
    for d in range(2):
        arrived(a_part(1 + d, 1 - d), a_ss.at[d, 1], a_rs.at[d, 1])
    for n in range(5):
        unit(n, stages[1])
    relay(15)
    for d in range(2):
        arrived(a_part(3, d), a_ss.at[d, 2], a_rs.at[d, 2])
    for n in range(5):
        unit(n, stages[2])
    relay(16)
    for n in range(5, 7):
        unit(n, whole)
    relay(18)
    unit(7, whole)
    chip_sum(*pending.pop(0))

    mine = pl.ds(pl.multiple_of(y * cols, cols), cols)
    for index in (1, 2, 0):
        span = stages[index]
        for k in range(NX):
            for c in range(NC):
                if k or c:
                    from_x, from_core = (x + k) % NX, (core + c) % NC
                    arrived(
                        xrecv.at[from_x, from_core, pl.ds(span[0], span[1] - span[0])],
                        x_ss.at[0, index],
                        x_rs.at[from_x, from_core, index],
                    )
        for t in range(*span):
            parts = []
            for c in range(NC):
                value = xrecv[0, c, t].astype(F32)
                for j in range(1, NX):
                    value = value + xrecv[j, c, t].astype(F32)
                parts.append(value.astype(BF16))
            tile = jnp.concatenate(parts, axis=0)
            if t:
                fsend[t - 1] = tile
                send(
                    fsend.at[t - 1],
                    out_ref.at[:, mine],
                    f_ss.at[t - 1],
                    f_rs.at[t - 1],
                    device(dy=turns[t]),
                )
            else:
                out_ref[:, mine] = tile
    for t in range(1, NY):
        source = (y - turns[t]) % NY
        lanes = pl.ds(pl.multiple_of(source * cols, cols), cols)
        arrived(out_ref.at[:, lanes], f_ss.at[t - 1], f_rs.at[t - 1])
    for copy in sends:
        copy.wait_send()
    for n in range(NZ):
        to_x, to_core = owner(n)

        @pl.when((to_x != x) | (to_core != core))
        def _():
            for index in range(3):
                owner_copy(n, index).wait_send()


def shards(
    x_in, multiplier_channels, b_proj, c_proj, dt_raw, dt_bias, a_log, skip_d, norm_gain, w_out
):
    tokens, channels = x_in.shape
    depth, cols = w_out.shape
    pair = channels // NY
    size = STATE // NZ
    vmem = pl.BlockSpec(memory_space=pltpu.VMEM)
    dma = pltpu.SemaphoreType.DMA
    half = cols // 2
    share = tokens // NC
    scratch = [
        pltpu.VMEM((NZ, 2, depth, half), BF16),
        pltpu.VMEM((NY, tokens, channels), BF16),
        pltpu.VMEM((tokens, channels), F32),
        pltpu.VMEM((tokens, channels), F32),
        pltpu.VMEM((NY - 1, STATE, pair), F32),
        pltpu.VMEM((NY, STATE, pair), BF16),
        pltpu.VMEM((NY, STATE, pair), BF16),
        pltpu.VMEM((NY, 8, pair), F32),
        pltpu.VMEM((NY, 8, pair), F32),
        pltpu.VMEM((NZ, size, pair), BF16),
        pltpu.VMEM((NZ, size, pair), BF16),
        pltpu.VMEM((8, pair), F32),
        pltpu.VMEM((NZ, 8, pair), F32),
        pltpu.VMEM((NZ, size, pair), BF16),
        pltpu.VMEM((NZ, size, pair), BF16),
        pltpu.VMEM((NY, STATE, pair), BF16),
        pltpu.VMEM((NY, STATE, pair), BF16),
        pltpu.VMEM((NC, NZ, NY, share, cols), F32),
        pltpu.VMEM((NZ, NY, share, cols), F32),
        pltpu.VMEM((NZ, NY, share, cols), BF16),
        pltpu.VMEM((NX, NC, NY, share, cols), BF16),
        pltpu.VMEM((NY - 1, tokens, cols), BF16),
        dma((2,)),
        dma((2, 4, 4)), dma((2, 4, 4)),
        dma((3,)), dma((3,)), dma((3,)), dma((3,)),
        dma((7,)), dma((7,)), dma((7,)), dma((7,)),
        dma((7,)), dma((7,)),
        dma((3,)), dma((3,)),
        dma((2, 3)), dma((2, 3)),
        dma((NZ, 3)), dma((NZ, 3)),
        dma((NZ, 3)), dma((NX, NC, 3)),
        dma((NY - 1,)), dma((NY - 1,)),
    ]
    return pl.pallas_call(
        kernel,
        out_shape=jax.ShapeDtypeStruct((tokens, channels), BF16),
        in_specs=[vmem] * 9 + [pl.BlockSpec(memory_space=pl.ANY)],
        out_specs=vmem,
        scratch_shapes=scratch,
        compiler_params=pltpu.CompilerParams(
            collective_id=0, has_side_effects=True, vmem_limit_bytes=56 * 1024 * 1024
        ),
        name="mixer",
    )(
        dt_raw.T,
        dt_bias.reshape(1, -1),
        a_log.reshape(1, -1),
        skip_d.reshape(1, -1),
        norm_gain.reshape(1, -1),
        b_proj,
        c_proj,
        x_in,
        multiplier_channels,
        w_out,
    )


def solution(mesh):
    return jax.shard_map(
        shards,
        mesh=mesh,
        in_specs=(
            P("seq", "grp"),
            P("seq", "grp"),
            P("seq", "grp"),
            P("seq", "grp"),
            P("seq", "grp"),
            P("grp"),
            P("grp"),
            P("grp"),
            P("grp"),
            P("grp", "seq"),
        ),
        out_specs=P("seq", "grp"),
        check_vma=False,
    )
```

```python
import jax
import jax.numpy as jnp
from jax import lax
from jax.experimental import pallas as pl
from jax.experimental.pallas import tpu as pltpu
from jax.sharding import PartitionSpec as P

MESH = pl.DeviceIdType.MESH
HIGH = lax.Precision.HIGHEST
WIDTH = 128
STATE = 128
NZ, NY, NX, NC = 8, 4, 4, 2
F32 = jnp.float32
BF16 = jnp.bfloat16


def split(value):
    high = value.astype(BF16)
    return high, (value - high.astype(F32)).astype(BF16)


def dot(a, b, dims=((1,), (0,))):
    return lax.dot_general(a, b, (dims, ((), ())), preferred_element_type=F32)


def kernel(
    dt_ref, bias_ref, alog_ref, skip_ref, gain_ref, b_ref, c_ref, x_hbm, m_hbm, w_ref,
    out_ref,
    x_ref, m_ref, wall, abuf, ybuf, smbuf, qbuf,
    lsend, lrecv, tsend, trecv,
    rsend, rrecv, dsend, drecv,
    esend, erecv, ssend, srecv,
    part_sums, precv, xsend, xrecv, fsend,
    in_sems, w_local, w_ss, w_rs, l_ss, l_rs, t_ss, t_rs, r_ss, r_rs, d_ss, d_rs,
    e_ss, e_rs, s_ss, s_rs, a_ss, a_rs, p_ss, p_rs, x_ss, x_rs, f_ss, f_rs,
):
    seq, grp = lax.axis_index("seq"), lax.axis_index("grp")
    z, y = seq // NY, seq % NY
    x, core = grp // NC, grp % NC
    tokens, channels = x_ref.shape
    heads = channels // WIDTH
    pair = channels // NY
    cols = w_ref.shape[1]
    khalf = w_ref.shape[0] // 2
    chalf = cols // 2
    thalf = tokens // 2
    share = tokens // NC

    def device(dz=0, dy=0, dx=0, dc=0):
        return (
            ((z + dz) % NZ) * NY + (y + dy) % NY,
            ((x + dx) % NX) * NC + (core + dc) % NC,
        )

    def remote(src, dst, ss, rs, to):
        return pltpu.make_async_remote_copy(
            src_ref=src, dst_ref=dst, send_sem=ss, recv_sem=rs, device_id=to, device_id_type=MESH
        )

    sends = []

    def send(src, dst, ss, rs, to):
        copy = remote(src, dst, ss, rs, to)
        copy.start()
        sends.append(copy)

    def arrived(dst, ss, rs):
        remote(dst, dst, ss, rs, device(dz=1)).wait_recv()

    barrier = pltpu.get_barrier_semaphore()
    others = (
        [dict(dz=k) for k in range(1, NZ)]
        + [dict(dy=k) for k in range(1, NY)]
        + [dict(dx=k, dc=c) for k in range(NX) for c in range(NC) if k or c]
    )
    for other in others:
        pl.semaphore_signal(barrier, inc=1, device_id=device(**other), device_id_type=MESH)
    own_w = []
    for i in range(2):
        copy = pltpu.make_async_copy(
            w_ref.at[:, i * chalf : (i + 1) * chalf], wall.at[z, i], w_local.at[i]
        )
        copy.start()
        own_w.append(copy)
    loads = [
        pltpu.make_async_copy(x_hbm, x_ref, in_sems.at[0]),
        pltpu.make_async_copy(m_hbm, m_ref, in_sems.at[1]),
    ]
    for copy in loads:
        copy.start()

    pl.semaphore_wait(barrier, len(others))

    def w_part(origin, d, i):
        half = i % 2 if d == 0 else 1 - i % 2
        return wall.at[origin, i // 2, pl.ds(half * khalf, khalf), :]

    last = NZ // 2
    items = [(step, i) for step in range(last) for i in range(4)] + [(last, 0), (last, 2)]
    done = [0]

    def relay(count):
        while done[0] < count:
            step, i = items[done[0]]
            done[0] += 1
            for d, sign in enumerate((1, -1)):
                part = source = w_part((z - sign * step) % NZ, d, i)
                if not step:
                    half = i % 2 if d == 0 else 1 - i % 2
                    source = w_ref.at[
                        pl.ds(half * khalf, khalf), pl.ds(i // 2 * chalf, chalf)
                    ]
                else:
                    arrived(part, w_ss.at[d, step - 1, i], w_rs.at[d, step - 1, i])
                if step < last - 1 or (step == last - 1 and i % 2 == 0):
                    send(source, part, w_ss.at[d, step, i], w_rs.at[d, step, i], device(dz=sign))

    relay(3)

    raw = jnp.transpose(dt_ref[...]) + bias_ref[...]
    dt = jnp.maximum(raw, 0.0) + jnp.log1p(jnp.exp(-jnp.abs(raw)))
    la = -jnp.exp(alog_ref[...]) * dt
    rows = lax.broadcasted_iota(jnp.int32, (tokens, tokens), 0)
    columns = lax.broadcasted_iota(jnp.int32, (tokens, tokens), 1)
    mask = rows >= columns
    cum = lax.dot_general(
        mask.astype(F32), la, (((1,), (0,)), ((), ())), precision=HIGH, preferred_element_type=F32
    )
    total = cum[tokens - 1 : tokens, :]
    weight = jnp.exp(total - cum) * dt

    for copy in loads + own_w:
        copy.wait()
    bmat, cmat = b_ref[...], c_ref[...]
    for j in range(NY):
        parts = []
        for h in range(j * heads // NY, (j + 1) * heads // NY):
            xh = x_ref[:, h * WIDTH : (h + 1) * WIDTH].astype(F32)
            parts.append(xh * weight[:, h : h + 1])
        high, low = split(jnp.concatenate(parts, axis=1))
        state = dot(bmat, high, ((0,), (0,))) + dot(bmat, low, ((0,), (0,)))
        lsend[j] = state.astype(BF16)
        tsend[j] = jnp.concatenate(
            [
                jnp.broadcast_to(total[:, h : h + 1], (8, WIDTH))
                for h in range(j * heads // NY, (j + 1) * heads // NY)
            ],
            axis=1,
        )
    logits = dot(cmat, bmat, ((1,), (1,)))
    cum_t = jnp.transpose(cum)
    dt_t = jnp.transpose(dt)
    for h in range(heads):
        span = slice(h * WIDTH, (h + 1) * WIDTH)
        decay = jnp.exp(jnp.where(mask, cum[:, h : h + 1] - cum_t[h : h + 1, :], -1e30))
        high, low = split(decay * logits * dt_t[h : h + 1, :])
        xh = x_ref[:, span]
        ybuf[:, span] = dot(high, xh) + dot(low, xh) + skip_ref[:, h : h + 1] * xh.astype(F32)
        gate = m_ref[:, span].astype(F32)
        smbuf[:, span] = gate / (1.0 + jnp.exp(-gate))

    for k in range(1, NY):
        to = (y + k) % NY
        send(lsend.at[to], lrecv.at[y], l_ss.at[k - 1], l_rs.at[k - 1], device(dy=k))
        send(tsend.at[to, pl.ds(0, 1), :], trecv.at[y, pl.ds(0, 1), :], t_ss.at[k - 1], t_rs.at[k - 1], device(dy=k))
    lrecv[y] = lsend[y]
    trecv[y] = tsend[y]

    for k in range(1, NY):
        source = (y - k) % NY
        arrived(lrecv.at[source], l_ss.at[k - 1], l_rs.at[k - 1])
        arrived(trecv.at[source, pl.ds(0, 1), :], t_ss.at[k - 1], t_rs.at[k - 1])
    before = [jnp.zeros((1, pair), F32)]
    current = lrecv[0].astype(F32)
    for j in range(NY):
        before.append(before[-1] + trecv[j][0:1, :])
        if j:
            qbuf[j - 1] = current
            current = jnp.exp(trecv[j][0:1, :]) * current + lrecv[j].astype(F32)
    size = STATE // NZ
    for k in range(NZ):
        rsend[k] = current[k * size : (k + 1) * size, :].astype(BF16)
    dsend[...] = jnp.broadcast_to(before[NY], (8, pair))
    for k in range(1, NZ):
        to = (z + k) % NZ
        send(rsend.at[to], rrecv.at[z], r_ss.at[k - 1], r_rs.at[k - 1], device(dz=k))
        send(dsend.at[pl.ds(0, 1), :], drecv.at[z, pl.ds(0, 1), :], d_ss.at[k - 1], d_rs.at[k - 1], device(dz=k))
    rrecv[z] = rsend[z]
    drecv[z] = dsend[...]
    relay(5)

    for k in range(1, NZ):
        source = (z - k) % NZ
        arrived(rrecv.at[source], r_ss.at[k - 1], r_rs.at[k - 1])
        arrived(drecv.at[source, pl.ds(0, 1), :], d_ss.at[k - 1], d_rs.at[k - 1])
    current = jnp.zeros((size, pair), F32)
    for k in range(NZ):
        esend[k] = current.astype(BF16)
        current = jnp.exp(drecv[k][0:1, :]) * current + rrecv[k].astype(F32)
    for k in range(1, NZ):
        to = (z + k) % NZ
        send(esend.at[to], erecv.at[z], e_ss.at[k - 1], e_rs.at[k - 1], device(dz=k))
    erecv[z] = esend[z]
    relay(8)
    for k in range(1, NZ):
        source = (z - k) % NZ
        arrived(erecv.at[source], e_ss.at[k - 1], e_rs.at[k - 1])
    entry = jnp.concatenate([erecv[k].astype(F32) for k in range(NZ)], axis=0)
    ssend[0] = entry.astype(BF16)
    for j in range(1, NY):
        ssend[j] = (qbuf[j - 1] + jnp.exp(before[j]) * entry).astype(BF16)
    for k in range(1, NY):
        to = (y + k) % NY
        send(ssend.at[to], srecv.at[y], s_ss.at[k - 1], s_rs.at[k - 1], device(dy=k))
    srecv[y] = ssend[y]
    relay(10)
    for k in range(1, NY):
        source = (y - k) % NY
        arrived(srecv.at[source], s_ss.at[k - 1], s_rs.at[k - 1])

    grown = jnp.exp(cum)
    squares = jnp.zeros((tokens, WIDTH), F32)
    for j in range(NY):
        inter = dot(cmat, srecv[j])
        for i in range(heads // NY):
            h = j * heads // NY + i
            span = slice(h * WIDTH, (h + 1) * WIDTH)
            value = ybuf[:, span] + grown[:, h : h + 1] * inter[:, i * WIDTH : (i + 1) * WIDTH]
            value = value * smbuf[:, span]
            ybuf[:, span] = value
            squares = squares + value * value
    mean = jnp.sum(squares, axis=1, keepdims=True) * (1.0 / channels)
    scale = lax.rsqrt(mean + 1e-05)
    abuf[0] = (ybuf[...] * scale * gain_ref[...]).astype(BF16)

    turns = (0, -1, 1, 2)

    def a_part(turn, half):
        return abuf.at[turn, pl.ds(half * thalf, thalf), :]

    for i in range(2):
        for d, sign in enumerate((1, -1)):
            half = i if d == 0 else 1 - i
            send(
                a_part(0, half),
                a_part(1 + d, half),
                a_ss.at[d, i],
                a_rs.at[d, i],
                device(dy=sign),
            )

    distances = (0, 1, -1, 2, -2, 3, -3, 4)
    stages = ((0, 1), (1, 3), (3, 4))
    whole = (0, NY)

    def owner(n):
        origin = (z + distances[n]) % NZ
        return origin // NC, origin % NC

    def lanes_of(half):
        return pl.ds(0, cols) if half is None else pl.ds(half * chalf, chalf)

    def index_of(span, half):
        return (half or 0) if span == whole else stages.index(span)

    def partner_copy(n, span, half):
        rows = pl.ds(span[0], span[1] - span[0])
        index = index_of(span, half)
        return (
            part_sums.at[1 - core, n, rows, :, lanes_of(half)],
            precv.at[n, rows, :, lanes_of(half)],
            p_ss.at[n, index],
            p_rs.at[n, index],
        )

    def multiply(n, span, half):
        origin = (z + distances[n]) % NZ
        if half is None:
            part = jnp.concatenate([wall[origin, 0], wall[origin, 1]], axis=1)
        else:
            part = wall[origin, half]
        width = part.shape[1]
        step = min(2, span[1] - span[0])
        for first in range(span[0], span[1], step):
            a = abuf[first : first + step].reshape(step * tokens, channels)
            total = dot(a, part).reshape(step, tokens, width)
            for c in range(NC):
                part_sums[c, n, first : first + step, :, lanes_of(half)] = total[
                    :, c * share : (c + 1) * share, :
                ]
        send(*partner_copy(n, span, half), device(dc=1))

    def owner_copy(n, span, half):
        rows = pl.ds(span[0], span[1] - span[0])
        to_x, to_core = owner(n)
        return remote(
            xsend.at[n, rows, :, lanes_of(half)],
            xrecv.at[x, core, rows, :, lanes_of(half)],
            x_ss.at[n, index_of(span, half)],
            x_rs.at[x, core],
            (seq, to_x * NC + to_core),
        )

    def chip_sum(n, span, half):
        to_x, to_core = owner(n)
        own = (to_x == x) & (to_core == core)
        _, dst, ss, rs = partner_copy(n, span, half)
        arrived(dst, ss, rs)
        at = (slice(*span), slice(None), lanes_of(half))
        both = part_sums[(core, n) + at] + precv[(n,) + at]
        xsend[(n,) + at] = both.astype(BF16)

        @pl.when(own)
        def _():
            xrecv[(x, core) + at] = xsend[(n,) + at]

        @pl.when(jnp.logical_not(own))
        def _():
            owner_copy(n, span, half).start()

    pending = []

    units = []

    def unit(n, span, half=None):
        multiply(n, span, half)
        units.append((n, span, half))
        pending.append((n, span, half))
        if len(pending) > 1:
            chip_sum(*pending.pop(0))

    relay(11)
    for n in range(3):
        unit(n, stages[0])
    relay(12)
    for d, sign in enumerate((1, -1)):
        arrived(a_part(1 + d, d), a_ss.at[d, 0], a_rs.at[d, 0])
        send(a_part(1 + d, d), a_part(3, d), a_ss.at[d, 2], a_rs.at[d, 2], device(dy=sign))
    relay(13)
    for n in range(3, 5):
        unit(n, stages[0])
    for d in range(2):
        arrived(a_part(1 + d, 1 - d), a_ss.at[d, 1], a_rs.at[d, 1])
    for n in range(5):
        unit(n, stages[1])
    relay(15)
    for d in range(2):
        arrived(a_part(3, d), a_ss.at[d, 2], a_rs.at[d, 2])
    for n in range(5):
        unit(n, stages[2])
    relay(16)
    for n in range(5, 7):
        unit(n, whole)
    relay(17)
    unit(7, whole, 0)
    relay(18)
    unit(7, whole, 1)
    chip_sum(*pending.pop(0))

    mine = pl.ds(pl.multiple_of(y * cols, cols), cols)
    for k in range(NX):
        for c in range(NC):
            if k or c:
                from_x, from_core = (x + k) % NX, (core + c) % NC
                arrived(xrecv.at[from_x, from_core], x_ss.at[0, 0], x_rs.at[from_x, from_core])
    for t in (3, 1, 2, 0):
        parts = []
        for c in range(NC):
            value = xrecv[0, c, t].astype(F32)
            for j in range(1, NX):
                value = value + xrecv[j, c, t].astype(F32)
            parts.append(value.astype(BF16))
        tile = jnp.concatenate(parts, axis=0)
        if t:
            fsend[t - 1] = tile
            send(
                fsend.at[t - 1],
                out_ref.at[:, mine],
                f_ss.at[t - 1],
                f_rs.at[t - 1],
                device(dy=turns[t]),
            )
        else:
            out_ref[:, mine] = tile
    for t in range(1, NY):
        source = (y - turns[t]) % NY
        lanes = pl.ds(pl.multiple_of(source * cols, cols), cols)
        arrived(out_ref.at[:, lanes], f_ss.at[t - 1], f_rs.at[t - 1])
    for copy in sends:
        copy.wait_send()
    for n in range(NZ):
        to_x, to_core = owner(n)

        @pl.when((to_x != x) | (to_core != core))
        def _():
            for other in units:
                if other[0] == n:
                    owner_copy(*other).wait_send()


def shards(
    x_in, multiplier_channels, b_proj, c_proj, dt_raw, dt_bias, a_log, skip_d, norm_gain, w_out
):
    tokens, channels = x_in.shape
    depth, cols = w_out.shape
    pair = channels // NY
    size = STATE // NZ
    vmem = pl.BlockSpec(memory_space=pltpu.VMEM)
    dma = pltpu.SemaphoreType.DMA
    half = cols // 2
    share = tokens // NC
    scratch = [
        pltpu.VMEM((tokens, channels), BF16),
        pltpu.VMEM((tokens, channels), BF16),
        pltpu.VMEM((NZ, 2, depth, half), BF16),
        pltpu.VMEM((NY, tokens, channels), BF16),
        pltpu.VMEM((tokens, channels), F32),
        pltpu.VMEM((tokens, channels), F32),
        pltpu.VMEM((NY - 1, STATE, pair), F32),
        pltpu.VMEM((NY, STATE, pair), BF16),
        pltpu.VMEM((NY, STATE, pair), BF16),
        pltpu.VMEM((NY, 8, pair), F32),
        pltpu.VMEM((NY, 8, pair), F32),
        pltpu.VMEM((NZ, size, pair), BF16),
        pltpu.VMEM((NZ, size, pair), BF16),
        pltpu.VMEM((8, pair), F32),
        pltpu.VMEM((NZ, 8, pair), F32),
        pltpu.VMEM((NZ, size, pair), BF16),
        pltpu.VMEM((NZ, size, pair), BF16),
        pltpu.VMEM((NY, STATE, pair), BF16),
        pltpu.VMEM((NY, STATE, pair), BF16),
        pltpu.VMEM((NC, NZ, NY, share, cols), F32),
        pltpu.VMEM((NZ, NY, share, cols), F32),
        pltpu.VMEM((NZ, NY, share, cols), BF16),
        pltpu.VMEM((NX, NC, NY, share, cols), BF16),
        pltpu.VMEM((NY - 1, tokens, cols), BF16),
        dma((2,)),
        dma((2,)),
        dma((2, 4, 4)), dma((2, 4, 4)),
        dma((3,)), dma((3,)), dma((3,)), dma((3,)),
        dma((7,)), dma((7,)), dma((7,)), dma((7,)),
        dma((7,)), dma((7,)),
        dma((3,)), dma((3,)),
        dma((2, 3)), dma((2, 3)),
        dma((NZ, 3)), dma((NZ, 3)),
        dma((NZ, 3)), dma((NX, NC)),
        dma((NY - 1,)), dma((NY - 1,)),
    ]
    return pl.pallas_call(
        kernel,
        out_shape=pltpu.VMEM((tokens, channels), BF16),
        in_specs=[vmem] * 7 + [pl.BlockSpec(memory_space=pl.ANY)] * 3,
        out_specs=vmem,
        scratch_shapes=scratch,
        compiler_params=pltpu.CompilerParams(
            collective_id=0, has_side_effects=True, vmem_limit_bytes=56 * 1024 * 1024
        ),
        name="mixer",
    )(
        dt_raw.T,
        dt_bias.reshape(1, -1),
        a_log.reshape(1, -1),
        skip_d.reshape(1, -1),
        norm_gain.reshape(1, -1),
        b_proj,
        c_proj,
        x_in,
        multiplier_channels,
        w_out,
    )


def solution(mesh):
    return jax.shard_map(
        shards,
        mesh=mesh,
        in_specs=(
            P("seq", "grp"),
            P("seq", "grp"),
            P("seq", "grp"),
            P("seq", "grp"),
            P("seq", "grp"),
            P("grp"),
            P("grp"),
            P("grp"),
            P("grp"),
            P("grp", "seq"),
        ),
        out_specs=P("seq", "grp"),
        check_vma=False,
    )
```

```python
import jax
import jax.numpy as jnp
from jax import lax
from jax.experimental import pallas as pl
from jax.experimental.pallas import tpu as pltpu
from jax.sharding import PartitionSpec as P

MESH = pl.DeviceIdType.MESH
HIGH = lax.Precision.HIGHEST
WIDTH = 128
STATE = 128
NZ, NY, NX, NC = 8, 4, 4, 2
F32 = jnp.float32
BF16 = jnp.bfloat16


def split(value):
    high = value.astype(BF16)
    return high, (value - high.astype(F32)).astype(BF16)


def dot(a, b, dims=((1,), (0,))):
    return lax.dot_general(a, b, (dims, ((), ())), preferred_element_type=F32)


def kernel(
    dt_ref, bias_ref, alog_ref, skip_ref, gain_ref, b_ref, c_ref, x_hbm, m_hbm, w_ref,
    out_ref,
    x_ref, m_ref, wall, abuf, ybuf, smbuf, qbuf,
    lsend, lrecv, tsend, trecv,
    rsend, rrecv, dsend, drecv,
    esend, erecv, ssend, srecv,
    part_sums, precv, xsend, xrecv, fsend,
    in_sems, w_local, w_ss, w_rs, l_ss, l_rs, t_ss, t_rs, r_ss, r_rs, d_ss, d_rs,
    e_ss, e_rs, s_ss, s_rs, a_ss, a_rs, p_ss, p_rs, x_ss, x_rs, f_ss, o_ss, f_rs,
):
    seq, grp = lax.axis_index("seq"), lax.axis_index("grp")
    z, y = seq // NY, seq % NY
    x, core = grp // NC, grp % NC
    tokens, channels = x_ref.shape
    heads = channels // WIDTH
    pair = channels // NY
    cols = w_ref.shape[1]
    khalf = w_ref.shape[0] // 2
    chalf = cols // 2
    thalf = tokens // 2
    share = tokens // NC

    def device(dz=0, dy=0, dx=0, dc=0):
        return (
            ((z + dz) % NZ) * NY + (y + dy) % NY,
            ((x + dx) % NX) * NC + (core + dc) % NC,
        )

    def remote(src, dst, ss, rs, to):
        return pltpu.make_async_remote_copy(
            src_ref=src, dst_ref=dst, send_sem=ss, recv_sem=rs, device_id=to, device_id_type=MESH
        )

    def send(src, dst, ss, rs, to):
        remote(src, dst, ss, rs, to).start()

    def sent(like, ss):
        remote(like, like, ss, f_rs, device(dz=1)).wait_send()

    def arrived(like, rs):
        remote(like, like, w_ss, rs, device(dz=1)).wait_recv()

    barrier = pltpu.get_barrier_semaphore()
    others = (
        [dict(dz=k) for k in range(1, NZ)]
        + [dict(dy=k) for k in range(1, NY)]
        + [dict(dx=k, dc=c) for k in range(NX) for c in range(NC) if k or c]
    )
    for other in others:
        pl.semaphore_signal(barrier, inc=1, device_id=device(**other), device_id_type=MESH)
    own_w = []
    for i in range(2):
        copy = pltpu.make_async_copy(
            w_ref.at[:, i * chalf : (i + 1) * chalf], wall.at[z, i], w_local.at[i]
        )
        copy.start()
        own_w.append(copy)
    loads = [
        pltpu.make_async_copy(x_hbm, x_ref, in_sems.at[0]),
        pltpu.make_async_copy(m_hbm, m_ref, in_sems.at[1]),
    ]
    for copy in loads:
        copy.start()

    pl.semaphore_wait(barrier, len(others))

    def w_part(origin, d, i):
        half = i % 2 if d == 0 else 1 - i % 2
        return wall.at[origin, i // 2, pl.ds(half * khalf, khalf), :]

    last = NZ // 2
    items = [(step, i) for step in range(last) for i in range(4)] + [(last, 0), (last, 2)]
    done = [0]

    def relay(count):
        while done[0] < count:
            step, i = items[done[0]]
            done[0] += 1
            for d, sign in enumerate((1, -1)):
                part = source = w_part((z - sign * step) % NZ, d, i)
                if not step:
                    half = i % 2 if d == 0 else 1 - i % 2
                    source = w_ref.at[
                        pl.ds(half * khalf, khalf), pl.ds(i // 2 * chalf, chalf)
                    ]
                else:
                    arrived(part, w_rs.at[d, step - 1, i])
                if step < last - 1 or (step == last - 1 and i % 2 == 0):
                    send(source, part, w_ss, w_rs.at[d, step, i], device(dz=sign))

    relay(3)

    raw = jnp.transpose(dt_ref[...]) + bias_ref[...]
    dt = jnp.maximum(raw, 0.0) + jnp.log1p(jnp.exp(-jnp.abs(raw)))
    la = -jnp.exp(alog_ref[...]) * dt
    rows = lax.broadcasted_iota(jnp.int32, (tokens, tokens), 0)
    columns = lax.broadcasted_iota(jnp.int32, (tokens, tokens), 1)
    mask = rows >= columns
    cum = lax.dot_general(
        mask.astype(F32), la, (((1,), (0,)), ((), ())), precision=HIGH, preferred_element_type=F32
    )
    total = cum[tokens - 1 : tokens, :]
    weight = jnp.exp(total - cum) * dt

    for copy in loads + own_w:
        copy.wait()
    bmat, cmat = b_ref[...], c_ref[...]
    for j in range(NY):
        parts = []
        for h in range(j * heads // NY, (j + 1) * heads // NY):
            xh = x_ref[:, h * WIDTH : (h + 1) * WIDTH].astype(F32)
            parts.append(xh * weight[:, h : h + 1])
        high, low = split(jnp.concatenate(parts, axis=1))
        state = dot(bmat, high, ((0,), (0,))) + dot(bmat, low, ((0,), (0,)))
        lsend[j] = state.astype(BF16)
        tsend[j] = jnp.concatenate(
            [
                jnp.broadcast_to(total[:, h : h + 1], (8, WIDTH))
                for h in range(j * heads // NY, (j + 1) * heads // NY)
            ],
            axis=1,
        )
    logits = dot(cmat, bmat, ((1,), (1,)))
    cum_t = jnp.transpose(cum)
    dt_t = jnp.transpose(dt)
    for h in range(heads):
        span = slice(h * WIDTH, (h + 1) * WIDTH)
        decay = jnp.exp(jnp.where(mask, cum[:, h : h + 1] - cum_t[h : h + 1, :], -1e30))
        high, low = split(decay * logits * dt_t[h : h + 1, :])
        xh = x_ref[:, span]
        ybuf[:, span] = dot(high, xh) + dot(low, xh) + skip_ref[:, h : h + 1] * xh.astype(F32)
        gate = m_ref[:, span].astype(F32)
        smbuf[:, span] = gate / (1.0 + jnp.exp(-gate))

    for k in range(1, NY):
        to = (y + k) % NY
        send(lsend.at[to], lrecv.at[y], l_ss, l_rs, device(dy=k))
        send(tsend.at[to, pl.ds(0, 1), :], trecv.at[y, pl.ds(0, 1), :], t_ss, t_rs, device(dy=k))
    lrecv[y] = lsend[y]
    trecv[y] = tsend[y]

    arrived(lrecv.at[pl.ds(0, NY - 1)], l_rs)
    arrived(trecv.at[pl.ds(0, NY - 1), pl.ds(0, 1), :], t_rs)
    before = [jnp.zeros((1, pair), F32)]
    current = lrecv[0].astype(F32)
    for j in range(NY):
        before.append(before[-1] + trecv[j][0:1, :])
        if j:
            qbuf[j - 1] = current
            current = jnp.exp(trecv[j][0:1, :]) * current + lrecv[j].astype(F32)
    size = STATE // NZ
    for k in range(NZ):
        rsend[k] = current[k * size : (k + 1) * size, :].astype(BF16)
    dsend[...] = jnp.broadcast_to(before[NY], (8, pair))
    for k in range(1, NZ):
        to = (z + k) % NZ
        send(rsend.at[to], rrecv.at[z], r_ss, r_rs, device(dz=k))
        send(dsend.at[pl.ds(0, 1), :], drecv.at[z, pl.ds(0, 1), :], d_ss, d_rs, device(dz=k))
    rrecv[z] = rsend[z]
    drecv[z] = dsend[...]
    relay(5)

    arrived(rrecv.at[pl.ds(0, NZ - 1)], r_rs)
    arrived(drecv.at[pl.ds(0, NZ - 1), pl.ds(0, 1), :], d_rs)
    current = jnp.zeros((size, pair), F32)
    for k in range(NZ):
        esend[k] = current.astype(BF16)
        current = jnp.exp(drecv[k][0:1, :]) * current + rrecv[k].astype(F32)
    for k in range(1, NZ):
        to = (z + k) % NZ
        send(esend.at[to], erecv.at[z], e_ss, e_rs, device(dz=k))
    erecv[z] = esend[z]
    relay(8)
    arrived(erecv.at[pl.ds(0, NZ - 1)], e_rs)
    entry = jnp.concatenate([erecv[k].astype(F32) for k in range(NZ)], axis=0)
    ssend[0] = entry.astype(BF16)
    for j in range(1, NY):
        ssend[j] = (qbuf[j - 1] + jnp.exp(before[j]) * entry).astype(BF16)
    for k in range(1, NY):
        to = (y + k) % NY
        send(ssend.at[to], srecv.at[y], s_ss, s_rs, device(dy=k))
    srecv[y] = ssend[y]
    relay(10)
    arrived(srecv.at[pl.ds(0, NY - 1)], s_rs)

    grown = jnp.exp(cum)
    squares = jnp.zeros((tokens, WIDTH), F32)
    for j in range(NY):
        inter = dot(cmat, srecv[j])
        for i in range(heads // NY):
            h = j * heads // NY + i
            span = slice(h * WIDTH, (h + 1) * WIDTH)
            value = ybuf[:, span] + grown[:, h : h + 1] * inter[:, i * WIDTH : (i + 1) * WIDTH]
            value = value * smbuf[:, span]
            ybuf[:, span] = value
            squares = squares + value * value
    mean = jnp.sum(squares, axis=1, keepdims=True) * (1.0 / channels)
    scale = lax.rsqrt(mean + 1e-05)
    abuf[0] = (ybuf[...] * scale * gain_ref[...]).astype(BF16)

    turns = (0, -1, 1, 2)

    def a_part(turn, half):
        return abuf.at[turn, pl.ds(half * thalf, thalf), :]

    for i in range(2):
        for d, sign in enumerate((1, -1)):
            half = i if d == 0 else 1 - i
            send(
                a_part(0, half),
                a_part(1 + d, half),
                a_ss,
                a_rs.at[d, i],
                device(dy=sign),
            )

    distances = (0, 1, -1, 2, -2, 3, -3, 4)
    stages = ((0, 1), (1, 3), (3, 4))
    whole = (0, NY)

    def owner(n):
        origin = (z + distances[n]) % NZ
        return origin // NC, origin % NC

    def lanes_of(half):
        return pl.ds(0, cols) if half is None else pl.ds(half * chalf, chalf)

    def index_of(span, half):
        return (half or 0) if span == whole else stages.index(span)

    def partner_copy(n, span, half):
        rows = pl.ds(span[0], span[1] - span[0])
        index = index_of(span, half)
        return (
            part_sums.at[1 - core, n, rows, :, lanes_of(half)],
            precv.at[n, rows, :, lanes_of(half)],
            p_ss,
            p_rs.at[n, index],
        )

    def multiply(n, span, half):
        origin = (z + distances[n]) % NZ
        if half is None:
            part = jnp.concatenate([wall[origin, 0], wall[origin, 1]], axis=1)
        else:
            part = wall[origin, half]
        width = part.shape[1]
        step = min(2, span[1] - span[0])
        for first in range(span[0], span[1], step):
            a = abuf[first : first + step].reshape(step * tokens, channels)
            total = dot(a, part).reshape(step, tokens, width)
            for c in range(NC):
                part_sums[c, n, first : first + step, :, lanes_of(half)] = total[
                    :, c * share : (c + 1) * share, :
                ]
        send(*partner_copy(n, span, half), device(dc=1))

    slab = share // NX

    def chip_sum(n, span, half):
        _, dst, _, rs = partner_copy(n, span, half)
        arrived(dst, rs)
        lanes = lanes_of(half)
        both = part_sums[core, n, span[0] : span[1], :, lanes]
        both = (both + precv[n, span[0] : span[1], :, lanes]).astype(BF16)
        for j in range(NX):
            xsend[n, j, span[0] : span[1], :, lanes] = both[:, j * slab : (j + 1) * slab, :]
        rows = pl.ds(span[0], span[1] - span[0])
        for k in range(1, NX):
            send(
                xsend.at[n, (x + k) % NX, rows, :, lanes],
                xrecv.at[n, k - 1, rows, :, lanes],
                x_ss,
                x_rs.at[n],
                device(dx=k),
            )

    mine = pl.ds(pl.multiple_of(y * cols, cols), cols)
    place = pl.ds(pl.multiple_of(core * share + x * slab, slab), slab)

    def finish(n):
        value = xsend[n, x].astype(F32)
        arrived(xrecv.at[n], x_rs.at[n])
        for k in range(1, NX):
            value = value + xrecv[n, k - 1].astype(F32)
        fsend[n] = value.astype(BF16)
        to_x, to_core = owner(n)
        for t in (3, 1, 2):
            to = (z * NY + (y + turns[t]) % NY, to_x * NC + to_core)
            send(fsend.at[n, t], out_ref.at[place, mine], f_ss, f_rs, to)
        own = (to_x == x) & (to_core == core)

        @pl.when(own)
        def _():
            pltpu.make_async_copy(fsend.at[n, 0], out_ref.at[place, mine], f_rs).start()

        @pl.when(jnp.logical_not(own))
        def _():
            send(
                fsend.at[n, 0], out_ref.at[place, mine], o_ss, f_rs, (seq, to_x * NC + to_core)
            )

    pending = []

    def unit(n, span, half=None):
        multiply(n, span, half)
        pending.append((n, span, half))
        if len(pending) > 1:
            chip_sum(*pending.pop(0))

    relay(11)
    for n in range(3):
        unit(n, stages[0])
    relay(12)
    for d, sign in enumerate((1, -1)):
        arrived(a_part(1 + d, d), a_rs.at[d, 0])
        send(a_part(1 + d, d), a_part(3, d), a_ss, a_rs.at[d, 2], device(dy=sign))
    relay(13)
    for n in range(3, 5):
        unit(n, stages[0])
    for d in range(2):
        arrived(a_part(1 + d, 1 - d), a_rs.at[d, 1])
    for n in range(5):
        unit(n, stages[1])
    relay(15)
    sent(lsend.at[pl.ds(0, NY - 1)], l_ss)
    sent(tsend.at[pl.ds(0, NY - 1), pl.ds(0, 1), :], t_ss)
    sent(rsend.at[pl.ds(0, NZ - 1)], r_ss)
    sent(drecv.at[pl.ds(0, NZ - 1), pl.ds(0, 1), :], d_ss)
    sent(esend.at[pl.ds(0, NZ - 1)], e_ss)
    sent(ssend.at[pl.ds(0, NY - 1)], s_ss)
    for d in range(2):
        arrived(a_part(3, d), a_rs.at[d, 2])
    for n in range(5):
        unit(n, stages[2])
    relay(16)
    unit(5, whole)
    unit(6, whole)
    sent(abuf.at[pl.ds(0, 3)], a_ss)
    relay(17)
    unit(7, whole, 0)
    relay(18)
    unit(7, whole, 1)
    chip_sum(*pending.pop(0))
    for n in range(NZ - 1):
        finish(n)
    finish(NZ - 1)

    sent(wall.at[pl.ds(0, NZ - 1)], w_ss)
    sent(precv, p_ss)
    sent(xrecv, x_ss)
    arrived(out_ref, f_rs)
    sent(fsend.at[:, pl.ds(1, NY - 1)], f_ss)
    sent(fsend.at[pl.ds(0, NZ - 1), 0], o_ss)


def shards(
    x_in, multiplier_channels, b_proj, c_proj, dt_raw, dt_bias, a_log, skip_d, norm_gain, w_out
):
    tokens, channels = x_in.shape
    depth, cols = w_out.shape
    pair = channels // NY
    size = STATE // NZ
    vmem = pl.BlockSpec(memory_space=pltpu.VMEM)
    dma = pltpu.SemaphoreType.DMA
    half = cols // 2
    share = tokens // NC
    scratch = [
        pltpu.VMEM((tokens, channels), BF16),
        pltpu.VMEM((tokens, channels), BF16),
        pltpu.VMEM((NZ, 2, depth, half), BF16),
        pltpu.VMEM((NY, tokens, channels), BF16),
        pltpu.VMEM((tokens, channels), F32),
        pltpu.VMEM((tokens, channels), F32),
        pltpu.VMEM((NY - 1, STATE, pair), F32),
        pltpu.VMEM((NY, STATE, pair), BF16),
        pltpu.VMEM((NY, STATE, pair), BF16),
        pltpu.VMEM((NY, 8, pair), F32),
        pltpu.VMEM((NY, 8, pair), F32),
        pltpu.VMEM((NZ, size, pair), BF16),
        pltpu.VMEM((NZ, size, pair), BF16),
        pltpu.VMEM((8, pair), F32),
        pltpu.VMEM((NZ, 8, pair), F32),
        pltpu.VMEM((NZ, size, pair), BF16),
        pltpu.VMEM((NZ, size, pair), BF16),
        pltpu.VMEM((NY, STATE, pair), BF16),
        pltpu.VMEM((NY, STATE, pair), BF16),
        pltpu.VMEM((NC, NZ, NY, share, cols), F32),
        pltpu.VMEM((NZ, NY, share, cols), F32),
        pltpu.VMEM((NZ, NX, NY, share // NX, cols), BF16),
        pltpu.VMEM((NZ, NX - 1, NY, share // NX, cols), BF16),
        pltpu.VMEM((NZ, NY, share // NX, cols), BF16),
        dma((2,)),
        dma((2,)),
        dma, dma((2, 4, 4)),
        dma, dma, dma, dma,
        dma, dma, dma, dma,
        dma, dma,
        dma, dma,
        dma, dma((2, 3)),
        dma, dma((NZ, 3)),
        dma, dma((NZ,)),
        dma, dma, dma,
    ]
    return pl.pallas_call(
        kernel,
        out_shape=pltpu.VMEM((tokens, channels), BF16),
        in_specs=[vmem] * 7 + [pl.BlockSpec(memory_space=pl.ANY)] * 3,
        out_specs=vmem,
        scratch_shapes=scratch,
        compiler_params=pltpu.CompilerParams(
            collective_id=0, has_side_effects=True, vmem_limit_bytes=56 * 1024 * 1024
        ),
        name="mixer",
    )(
        dt_raw.T,
        dt_bias.reshape(1, -1),
        a_log.reshape(1, -1),
        skip_d.reshape(1, -1),
        norm_gain.reshape(1, -1),
        b_proj,
        c_proj,
        x_in,
        multiplier_channels,
        w_out,
    )


def solution(mesh):
    return jax.shard_map(
        shards,
        mesh=mesh,
        in_specs=(
            P("seq", "grp"),
            P("seq", "grp"),
            P("seq", "grp"),
            P("seq", "grp"),
            P("seq", "grp"),
            P("grp"),
            P("grp"),
            P("grp"),
            P("grp"),
            P("grp", "seq"),
        ),
        out_specs=P("seq", "grp"),
        check_vma=False,
    )
```

```python
import jax
import jax.numpy as jnp
from jax import lax
from jax.experimental import pallas as pl
from jax.experimental.pallas import tpu as pltpu
from jax.sharding import PartitionSpec as P

MESH = pl.DeviceIdType.MESH
HIGH = lax.Precision.HIGHEST
WIDTH = 128
STATE = 128
NZ, NY, NX, NC = 8, 4, 4, 2
F32 = jnp.float32
BF16 = jnp.bfloat16


def split(value):
    high = value.astype(BF16)
    return high, (value - high.astype(F32)).astype(BF16)


def dot(a, b, dims=((1,), (0,))):
    return lax.dot_general(a, b, (dims, ((), ())), preferred_element_type=F32)


def kernel(
    dt_hbm, bias_hbm, alog_hbm, skip_hbm, gain_hbm, b_hbm, c_hbm, x_hbm, m_hbm, w_ref,
    out_ref,
    dt_ref, bias_ref, alog_ref, skip_ref, gain_ref, b_ref, c_ref, x_ref, m_ref, wall, abuf, ybuf, smbuf, qbuf,
    lsend, lrecv, tsend, trecv,
    rsend, rrecv, dsend, drecv,
    esend, erecv, ssend, srecv,
    part_sums, precv, xsend, xrecv, fsend,
    in_sems, w_local, w_ss, w_rs, l_ss, l_rs, t_ss, t_rs, r_ss, r_rs, d_ss, d_rs,
    e_ss, e_rs, s_ss, s_rs, a_ss, a_rs, p_ss, p_rs, x_ss, x_rs, f_ss, o_ss, f_rs,
):
    seq, grp = lax.axis_index("seq"), lax.axis_index("grp")
    z, y = seq // NY, seq % NY
    x, core = grp // NC, grp % NC
    tokens, channels = x_ref.shape
    heads = channels // WIDTH
    pair = channels // NY
    cols = w_ref.shape[1]
    khalf = w_ref.shape[0] // 2
    chalf = cols // 2
    thalf = tokens // 2
    share = tokens // NC

    def device(dz=0, dy=0, dx=0, dc=0):
        return (
            ((z + dz) % NZ) * NY + (y + dy) % NY,
            ((x + dx) % NX) * NC + (core + dc) % NC,
        )

    def remote(src, dst, ss, rs, to):
        return pltpu.make_async_remote_copy(
            src_ref=src, dst_ref=dst, send_sem=ss, recv_sem=rs, device_id=to, device_id_type=MESH
        )

    def send(src, dst, ss, rs, to):
        remote(src, dst, ss, rs, to).start()

    def sent(like, ss):
        remote(like, like, ss, f_rs, device(dz=1)).wait_send()

    def arrived(like, rs):
        remote(like, like, w_ss, rs, device(dz=1)).wait_recv()

    barrier = pltpu.get_barrier_semaphore()
    others = (
        [dict(dz=k) for k in range(1, NZ)]
        + [dict(dy=k) for k in range(1, NY)]
        + [dict(dx=k, dc=c) for k in range(NX) for c in range(NC) if k or c]
    )
    for other in others:
        pl.semaphore_signal(barrier, inc=1, device_id=device(**other), device_id_type=MESH)
    own_w = []
    for i in range(2):
        copy = pltpu.make_async_copy(
            w_ref.at[:, i * chalf : (i + 1) * chalf], wall.at[z, i], w_local.at[i]
        )
        copy.start()
        own_w.append(copy)
    loads = [
        pltpu.make_async_copy(src, dst, in_sems.at[i])
        for i, (src, dst) in enumerate(
            (
                (dt_hbm, dt_ref),
                (bias_hbm, bias_ref),
                (alog_hbm, alog_ref),
                (x_hbm, x_ref),
                (b_hbm, b_ref),
                (c_hbm, c_ref),
                (skip_hbm, skip_ref),
                (m_hbm, m_ref),
                (gain_hbm, gain_ref),
            )
        )
    ]
    for copy in loads:
        copy.start()

    pl.semaphore_wait(barrier, len(others))

    def w_part(origin, d, i):
        half = i % 2 if d == 0 else 1 - i % 2
        return wall.at[origin, i // 2, pl.ds(half * khalf, khalf), :]

    last = NZ // 2
    items = [(step, i) for step in range(last) for i in range(4)] + [(last, 0), (last, 2)]
    done = [0]

    def relay(count):
        while done[0] < count:
            step, i = items[done[0]]
            done[0] += 1
            for d, sign in enumerate((1, -1)):
                part = source = w_part((z - sign * step) % NZ, d, i)
                if not step:
                    half = i % 2 if d == 0 else 1 - i % 2
                    source = w_ref.at[
                        pl.ds(half * khalf, khalf), pl.ds(i // 2 * chalf, chalf)
                    ]
                else:
                    arrived(part, w_rs.at[d, step - 1, i])
                if step < last - 1 or (step == last - 1 and i % 2 == 0):
                    send(source, part, w_ss, w_rs.at[d, step, i], device(dz=sign))

    relay(3)

    for copy in loads + own_w:
        copy.wait()
    raw = jnp.transpose(dt_ref[...]) + bias_ref[...]
    dt = jnp.maximum(raw, 0.0) + jnp.log1p(jnp.exp(-jnp.abs(raw)))
    la = -jnp.exp(alog_ref[...]) * dt
    rows = lax.broadcasted_iota(jnp.int32, (tokens, tokens), 0)
    columns = lax.broadcasted_iota(jnp.int32, (tokens, tokens), 1)
    mask = rows >= columns
    cum = lax.dot_general(
        mask.astype(F32), la, (((1,), (0,)), ((), ())), precision=HIGH, preferred_element_type=F32
    )
    total = cum[tokens - 1 : tokens, :]
    weight = jnp.exp(total - cum) * dt

    bmat, cmat = b_ref[...], c_ref[...]
    for j in range(NY):
        parts = []
        for h in range(j * heads // NY, (j + 1) * heads // NY):
            xh = x_ref[:, h * WIDTH : (h + 1) * WIDTH].astype(F32)
            parts.append(xh * weight[:, h : h + 1])
        high, low = split(jnp.concatenate(parts, axis=1))
        state = dot(bmat, high, ((0,), (0,))) + dot(bmat, low, ((0,), (0,)))
        lsend[j] = state.astype(BF16)
        tsend[j] = jnp.concatenate(
            [
                jnp.broadcast_to(total[:, h : h + 1], (8, WIDTH))
                for h in range(j * heads // NY, (j + 1) * heads // NY)
            ],
            axis=1,
        )
    logits = dot(cmat, bmat, ((1,), (1,)))
    cum_t = jnp.transpose(cum)
    dt_t = jnp.transpose(dt)
    for h in range(heads):
        span = slice(h * WIDTH, (h + 1) * WIDTH)
        decay = jnp.exp(jnp.where(mask, cum[:, h : h + 1] - cum_t[h : h + 1, :], -1e30))
        high, low = split(decay * logits * dt_t[h : h + 1, :])
        xh = x_ref[:, span]
        ybuf[:, span] = dot(high, xh) + dot(low, xh) + skip_ref[:, h : h + 1] * xh.astype(F32)
        gate = m_ref[:, span].astype(F32)
        smbuf[:, span] = gate / (1.0 + jnp.exp(-gate))

    for k in range(1, NY):
        to = (y + k) % NY
        send(lsend.at[to], lrecv.at[y], l_ss, l_rs, device(dy=k))
        send(tsend.at[to, pl.ds(0, 1), :], trecv.at[y, pl.ds(0, 1), :], t_ss, t_rs, device(dy=k))
    lrecv[y] = lsend[y]
    trecv[y] = tsend[y]

    arrived(lrecv.at[pl.ds(0, NY - 1)], l_rs)
    arrived(trecv.at[pl.ds(0, NY - 1), pl.ds(0, 1), :], t_rs)
    before = [jnp.zeros((1, pair), F32)]
    current = lrecv[0].astype(F32)
    for j in range(NY):
        before.append(before[-1] + trecv[j][0:1, :])
        if j:
            qbuf[j - 1] = current
            current = jnp.exp(trecv[j][0:1, :]) * current + lrecv[j].astype(F32)
    size = STATE // NZ
    for k in range(NZ):
        rsend[k] = current[k * size : (k + 1) * size, :].astype(BF16)
    dsend[...] = jnp.broadcast_to(before[NY], (8, pair))
    for k in range(1, NZ):
        to = (z + k) % NZ
        send(rsend.at[to], rrecv.at[z], r_ss, r_rs, device(dz=k))
        send(dsend.at[pl.ds(0, 1), :], drecv.at[z, pl.ds(0, 1), :], d_ss, d_rs, device(dz=k))
    rrecv[z] = rsend[z]
    drecv[z] = dsend[...]
    relay(5)

    arrived(rrecv.at[pl.ds(0, NZ - 1)], r_rs)
    arrived(drecv.at[pl.ds(0, NZ - 1), pl.ds(0, 1), :], d_rs)
    current = jnp.zeros((size, pair), F32)
    for k in range(NZ):
        esend[k] = current.astype(BF16)
        current = jnp.exp(drecv[k][0:1, :]) * current + rrecv[k].astype(F32)
    for k in range(1, NZ):
        to = (z + k) % NZ
        send(esend.at[to], erecv.at[z], e_ss, e_rs, device(dz=k))
    erecv[z] = esend[z]
    relay(8)
    arrived(erecv.at[pl.ds(0, NZ - 1)], e_rs)
    entry = jnp.concatenate([erecv[k].astype(F32) for k in range(NZ)], axis=0)
    ssend[0] = entry.astype(BF16)
    for j in range(1, NY):
        ssend[j] = (qbuf[j - 1] + jnp.exp(before[j]) * entry).astype(BF16)
    for k in range(1, NY):
        to = (y + k) % NY
        send(ssend.at[to], srecv.at[y], s_ss, s_rs, device(dy=k))
    srecv[y] = ssend[y]
    relay(11)
    arrived(srecv.at[pl.ds(0, NY - 1)], s_rs)

    grown = jnp.exp(cum)
    squares = jnp.zeros((tokens, WIDTH), F32)
    for j in range(NY):
        inter = dot(cmat, srecv[j])
        for i in range(heads // NY):
            h = j * heads // NY + i
            span = slice(h * WIDTH, (h + 1) * WIDTH)
            value = ybuf[:, span] + grown[:, h : h + 1] * inter[:, i * WIDTH : (i + 1) * WIDTH]
            value = value * smbuf[:, span]
            ybuf[:, span] = value
            squares = squares + value * value
    mean = jnp.sum(squares, axis=1, keepdims=True) * (1.0 / channels)
    scale = lax.rsqrt(mean + 1e-05)
    abuf[0] = (ybuf[...] * scale * gain_ref[...]).astype(BF16)

    turns = (0, -1, 1, 2)

    def a_part(turn, half):
        return abuf.at[turn, pl.ds(half * thalf, thalf), :]

    for i in range(2):
        for d, sign in enumerate((1, -1)):
            half = i if d == 0 else 1 - i
            send(
                a_part(0, half),
                a_part(1 + d, half),
                a_ss,
                a_rs.at[d, i],
                device(dy=sign),
            )

    distances = (0, 1, -1, 2, -2, 3, -3, 4)
    stages = ((0, 1), (1, 3), (3, 4))
    whole = (0, NY)

    def owner(n):
        origin = (z + distances[n]) % NZ
        return origin // NC, origin % NC

    def lanes_of(half):
        return pl.ds(0, cols) if half is None else pl.ds(half * chalf, chalf)

    def index_of(span, half):
        return (half or 0) if span == whole else stages.index(span)

    def partner_copy(n, span, half):
        rows = pl.ds(span[0], span[1] - span[0])
        index = index_of(span, half)
        return (
            part_sums.at[1 - core, n, rows, :, lanes_of(half)],
            precv.at[n, rows, :, lanes_of(half)],
            p_ss,
            p_rs.at[n, index],
        )

    def multiply(n, span, half):
        origin = (z + distances[n]) % NZ
        if half is None:
            part = jnp.concatenate([wall[origin, 0], wall[origin, 1]], axis=1)
        else:
            part = wall[origin, half]
        width = part.shape[1]
        step = min(2, span[1] - span[0])
        for first in range(span[0], span[1], step):
            a = abuf[first : first + step].reshape(step * tokens, channels)
            total = dot(a, part).reshape(step, tokens, width)
            for c in range(NC):
                part_sums[c, n, first : first + step, :, lanes_of(half)] = total[
                    :, c * share : (c + 1) * share, :
                ]
        send(*partner_copy(n, span, half), device(dc=1))

    slab = share // NX

    def chip_sum(n, span, half):
        _, dst, _, rs = partner_copy(n, span, half)
        arrived(dst, rs)
        lanes = lanes_of(half)
        both = part_sums[core, n, span[0] : span[1], :, lanes]
        both = (both + precv[n, span[0] : span[1], :, lanes]).astype(BF16)
        for j in range(NX):
            xsend[n, j, span[0] : span[1], :, lanes] = both[:, j * slab : (j + 1) * slab, :]
        rows = pl.ds(span[0], span[1] - span[0])
        for k in range(1, NX):
            send(
                xsend.at[n, (x + k) % NX, rows, :, lanes],
                xrecv.at[n, k - 1, rows, :, lanes],
                x_ss,
                x_rs.at[n],
                device(dx=k),
            )

    mine = pl.ds(pl.multiple_of(y * cols, cols), cols)
    place = pl.ds(pl.multiple_of(core * share + x * slab, slab), slab)

    def finish(n):
        value = xsend[n, x].astype(F32)
        arrived(xrecv.at[n], x_rs.at[n])
        for k in range(1, NX):
            value = value + xrecv[n, k - 1].astype(F32)
        fsend[n] = value.astype(BF16)
        to_x, to_core = owner(n)
        for t in (3, 1, 2):
            to = (z * NY + (y + turns[t]) % NY, to_x * NC + to_core)
            send(fsend.at[n, t], out_ref.at[place, mine], f_ss, f_rs, to)
        own = (to_x == x) & (to_core == core)

        @pl.when(own)
        def _():
            pltpu.make_async_copy(fsend.at[n, 0], out_ref.at[place, mine], f_rs).start()

        @pl.when(jnp.logical_not(own))
        def _():
            send(
                fsend.at[n, 0], out_ref.at[place, mine], o_ss, f_rs, (seq, to_x * NC + to_core)
            )

    pending = []

    def unit(n, span, half=None):
        multiply(n, span, half)
        pending.append((n, span, half))
        if len(pending) > 1:
            chip_sum(*pending.pop(0))

    relay(11)
    for n in range(3):
        unit(n, stages[0])
    relay(12)
    for d, sign in enumerate((1, -1)):
        arrived(a_part(1 + d, d), a_rs.at[d, 0])
        send(a_part(1 + d, d), a_part(3, d), a_ss, a_rs.at[d, 2], device(dy=sign))
    relay(13)
    for n in range(3, 5):
        unit(n, stages[0])
    for d in range(2):
        arrived(a_part(1 + d, 1 - d), a_rs.at[d, 1])
    for n in range(5):
        unit(n, stages[1])
    relay(15)
    sent(lsend.at[pl.ds(0, NY - 1)], l_ss)
    sent(tsend.at[pl.ds(0, NY - 1), pl.ds(0, 1), :], t_ss)
    sent(rsend.at[pl.ds(0, NZ - 1)], r_ss)
    sent(drecv.at[pl.ds(0, NZ - 1), pl.ds(0, 1), :], d_ss)
    sent(esend.at[pl.ds(0, NZ - 1)], e_ss)
    sent(ssend.at[pl.ds(0, NY - 1)], s_ss)
    for d in range(2):
        arrived(a_part(3, d), a_rs.at[d, 2])
    for n in range(5):
        unit(n, stages[2])
    relay(16)
    unit(5, whole)
    unit(6, whole)
    sent(abuf.at[pl.ds(0, 3)], a_ss)
    relay(17)
    unit(7, whole, 0)
    relay(18)
    unit(7, whole, 1)
    chip_sum(*pending.pop(0))
    for n in range(NZ - 1):
        finish(n)
    finish(NZ - 1)

    sent(wall.at[pl.ds(0, NZ - 1)], w_ss)
    sent(precv, p_ss)
    sent(xrecv, x_ss)
    arrived(out_ref, f_rs)
    sent(fsend.at[:, pl.ds(1, NY - 1)], f_ss)
    sent(fsend.at[pl.ds(0, NZ - 1), 0], o_ss)


def shards(
    x_in, multiplier_channels, b_proj, c_proj, dt_raw, dt_bias, a_log, skip_d, norm_gain, w_out
):
    tokens, channels = x_in.shape
    depth, cols = w_out.shape
    pair = channels // NY
    size = STATE // NZ
    vmem = pl.BlockSpec(memory_space=pltpu.VMEM)
    dma = pltpu.SemaphoreType.DMA
    half = cols // 2
    share = tokens // NC
    heads = channels // WIDTH
    scratch = [
        pltpu.VMEM((heads, tokens), F32),
        pltpu.VMEM((1, heads), F32),
        pltpu.VMEM((1, heads), F32),
        pltpu.VMEM((1, heads), F32),
        pltpu.VMEM((1, channels), F32),
        pltpu.VMEM((tokens, STATE), BF16),
        pltpu.VMEM((tokens, STATE), BF16),
        pltpu.VMEM((tokens, channels), BF16),
        pltpu.VMEM((tokens, channels), BF16),
        pltpu.VMEM((NZ, 2, depth, half), BF16),
        pltpu.VMEM((NY, tokens, channels), BF16),
        pltpu.VMEM((tokens, channels), F32),
        pltpu.VMEM((tokens, channels), F32),
        pltpu.VMEM((NY - 1, STATE, pair), F32),
        pltpu.VMEM((NY, STATE, pair), BF16),
        pltpu.VMEM((NY, STATE, pair), BF16),
        pltpu.VMEM((NY, 8, pair), F32),
        pltpu.VMEM((NY, 8, pair), F32),
        pltpu.VMEM((NZ, size, pair), BF16),
        pltpu.VMEM((NZ, size, pair), BF16),
        pltpu.VMEM((8, pair), F32),
        pltpu.VMEM((NZ, 8, pair), F32),
        pltpu.VMEM((NZ, size, pair), BF16),
        pltpu.VMEM((NZ, size, pair), BF16),
        pltpu.VMEM((NY, STATE, pair), BF16),
        pltpu.VMEM((NY, STATE, pair), BF16),
        pltpu.VMEM((NC, NZ, NY, share, cols), F32),
        pltpu.VMEM((NZ, NY, share, cols), F32),
        pltpu.VMEM((NZ, NX, NY, share // NX, cols), BF16),
        pltpu.VMEM((NZ, NX - 1, NY, share // NX, cols), BF16),
        pltpu.VMEM((NZ, NY, share // NX, cols), BF16),
        dma((9,)),
        dma((2,)),
        dma, dma((2, 4, 4)),
        dma, dma, dma, dma,
        dma, dma, dma, dma,
        dma, dma,
        dma, dma,
        dma, dma((2, 3)),
        dma, dma((NZ, 3)),
        dma, dma((NZ,)),
        dma, dma, dma,
    ]
    return pl.pallas_call(
        kernel,
        out_shape=pltpu.VMEM((tokens, channels), BF16),
        in_specs=[pl.BlockSpec(memory_space=pl.ANY)] * 10,
        out_specs=vmem,
        scratch_shapes=scratch,
        compiler_params=pltpu.CompilerParams(
            collective_id=0, has_side_effects=True, vmem_limit_bytes=56 * 1024 * 1024
        ),
        name="mixer",
    )(
        dt_raw.T,
        dt_bias.reshape(1, -1),
        a_log.reshape(1, -1),
        skip_d.reshape(1, -1),
        norm_gain.reshape(1, -1),
        b_proj,
        c_proj,
        x_in,
        multiplier_channels,
        w_out,
    )


def solution(mesh):
    return jax.shard_map(
        shards,
        mesh=mesh,
        in_specs=(
            P("seq", "grp"),
            P("seq", "grp"),
            P("seq", "grp"),
            P("seq", "grp"),
            P("seq", "grp"),
            P("grp"),
            P("grp"),
            P("grp"),
            P("grp"),
            P("grp", "seq"),
        ),
        out_specs=P("seq", "grp"),
        check_vma=False,
    )
```

```python
import jax
import jax.numpy as jnp
from jax import lax
from jax.experimental import pallas as pl
from jax.experimental.pallas import tpu as pltpu
from jax.sharding import PartitionSpec as P

MESH = pl.DeviceIdType.MESH
HIGH = lax.Precision.HIGHEST
WIDTH = 128
STATE = 128
NZ, NY, NX, NC = 8, 4, 4, 2
F32 = jnp.float32
BF16 = jnp.bfloat16


def split(value):
    high = value.astype(BF16)
    return high, (value - high.astype(F32)).astype(BF16)


def dot(a, b, dims=((1,), (0,))):
    return lax.dot_general(a, b, (dims, ((), ())), preferred_element_type=F32)


def kernel(
    dt_hbm, bias_hbm, alog_hbm, skip_hbm, gain_hbm, b_hbm, c_hbm, x_hbm, m_hbm, w_ref,
    out_ref,
    dt_ref, bias_ref, alog_ref, skip_ref, gain_ref, b_ref, c_ref, x_ref, m_ref, wall, abuf, ybuf, smbuf, qbuf,
    lsend, lrecv, tsend, trecv,
    rsend, rrecv, dsend, drecv,
    esend, erecv, ssend, srecv,
    part_sums, precv, xsend, xown, xrecv, fsend,
    in_sems, w_local, w_ss, w_rs, l_ss, l_rs, t_ss, t_rs, r_ss, r_rs, d_ss, d_rs,
    e_ss, e_rs, s_ss, s_rs, a_ss, a_rs, p_ss, p_rs, x_ss, x_rs, f_ss, o_ss, f_rs,
):
    seq, grp = lax.axis_index("seq"), lax.axis_index("grp")
    z, y = seq // NY, seq % NY
    x, core = grp // NC, grp % NC
    tokens, channels = x_ref.shape
    heads = channels // WIDTH
    pair = channels // NY
    cols = w_ref.shape[1]
    khalf = w_ref.shape[0] // 2
    chalf = cols // 2
    thalf = tokens // 2
    share = tokens // NC

    def device(dz=0, dy=0, dx=0, dc=0):
        return (
            ((z + dz) % NZ) * NY + (y + dy) % NY,
            ((x + dx) % NX) * NC + (core + dc) % NC,
        )

    def remote(src, dst, ss, rs, to):
        return pltpu.make_async_remote_copy(
            src_ref=src, dst_ref=dst, send_sem=ss, recv_sem=rs, device_id=to, device_id_type=MESH
        )

    def send(src, dst, ss, rs, to):
        remote(src, dst, ss, rs, to).start()

    def sent(like, ss):
        remote(like, like, ss, f_rs, device(dz=1)).wait_send()

    def arrived(like, rs):
        remote(like, like, w_ss, rs, device(dz=1)).wait_recv()

    barrier = pltpu.get_barrier_semaphore()
    others = (
        [dict(dz=k) for k in range(1, NZ)]
        + [dict(dy=k) for k in range(1, NY)]
        + [dict(dx=k, dc=c) for k in range(NX) for c in range(NC) if k or c]
    )
    for other in others:
        pl.semaphore_signal(barrier, inc=1, device_id=device(**other), device_id_type=MESH)
    own_w = []
    for i in range(2):
        copy = pltpu.make_async_copy(
            w_ref.at[:, i * chalf : (i + 1) * chalf], wall.at[z, i], w_local.at[i]
        )
        copy.start()
        own_w.append(copy)
    loads = [
        pltpu.make_async_copy(src, dst, in_sems.at[i])
        for i, (src, dst) in enumerate(
            (
                (dt_hbm, dt_ref),
                (bias_hbm, bias_ref),
                (alog_hbm, alog_ref),
                (x_hbm, x_ref),
                (b_hbm, b_ref),
                (c_hbm, c_ref),
                (skip_hbm, skip_ref),
                (m_hbm, m_ref),
                (gain_hbm, gain_ref),
            )
        )
    ]
    for copy in loads:
        copy.start()

    pl.semaphore_wait(barrier, len(others))

    def w_part(origin, d, i):
        half = i % 2 if d == 0 else 1 - i % 2
        return wall.at[origin, i // 2, pl.ds(half * khalf, khalf), :]

    last = NZ // 2
    items = [(step, i) for step in range(last) for i in range(4)] + [(last, 0), (last, 2)]
    done = [0]

    def relay(count):
        while done[0] < count:
            step, i = items[done[0]]
            done[0] += 1
            for d, sign in enumerate((1, -1)):
                part = source = w_part((z - sign * step) % NZ, d, i)
                if not step:
                    half = i % 2 if d == 0 else 1 - i % 2
                    source = w_ref.at[
                        pl.ds(half * khalf, khalf), pl.ds(i // 2 * chalf, chalf)
                    ]
                else:
                    arrived(part, w_rs.at[d, step - 1, i])
                if step < last - 1 or (step == last - 1 and i % 2 == 0):
                    send(source, part, w_ss, w_rs.at[d, step, i], device(dz=sign))

    relay(3)

    for copy in loads + own_w:
        copy.wait()
    raw = jnp.transpose(dt_ref[...]) + bias_ref[...]
    dt = jnp.maximum(raw, 0.0) + jnp.log1p(jnp.exp(-jnp.abs(raw)))
    la = -jnp.exp(alog_ref[...]) * dt
    rows = lax.broadcasted_iota(jnp.int32, (tokens, tokens), 0)
    columns = lax.broadcasted_iota(jnp.int32, (tokens, tokens), 1)
    mask = rows >= columns
    cum = lax.dot_general(
        mask.astype(F32), la, (((1,), (0,)), ((), ())), precision=HIGH, preferred_element_type=F32
    )
    total = cum[tokens - 1 : tokens, :]
    weight = jnp.exp(total - cum) * dt

    bmat, cmat = b_ref[...], c_ref[...]
    for j in range(NY):
        parts = []
        for h in range(j * heads // NY, (j + 1) * heads // NY):
            xh = x_ref[:, h * WIDTH : (h + 1) * WIDTH].astype(F32)
            parts.append(xh * weight[:, h : h + 1])
        high, low = split(jnp.concatenate(parts, axis=1))
        state = dot(bmat, high, ((0,), (0,))) + dot(bmat, low, ((0,), (0,)))
        lsend[j] = state.astype(BF16)
        tsend[j] = jnp.concatenate(
            [
                jnp.broadcast_to(total[:, h : h + 1], (8, WIDTH))
                for h in range(j * heads // NY, (j + 1) * heads // NY)
            ],
            axis=1,
        )
    logits = dot(cmat, bmat, ((1,), (1,)))
    cum_t = jnp.transpose(cum)
    dt_t = jnp.transpose(dt)
    for h in range(heads):
        span = slice(h * WIDTH, (h + 1) * WIDTH)
        decay = jnp.exp(jnp.where(mask, cum[:, h : h + 1] - cum_t[h : h + 1, :], -1e30))
        high, low = split(decay * logits * dt_t[h : h + 1, :])
        xh = x_ref[:, span]
        ybuf[:, span] = dot(high, xh) + dot(low, xh) + skip_ref[:, h : h + 1] * xh.astype(F32)
        gate = m_ref[:, span].astype(F32)
        smbuf[:, span] = gate / (1.0 + jnp.exp(-gate))

    for k in range(1, NY):
        to = (y + k) % NY
        send(lsend.at[to], lrecv.at[y], l_ss, l_rs, device(dy=k))
        send(tsend.at[to, pl.ds(0, 1), :], trecv.at[y, pl.ds(0, 1), :], t_ss, t_rs, device(dy=k))
    lrecv[y] = lsend[y]
    trecv[y] = tsend[y]

    arrived(lrecv.at[pl.ds(0, NY - 1)], l_rs)
    arrived(trecv.at[pl.ds(0, NY - 1), pl.ds(0, 1), :], t_rs)
    before = [jnp.zeros((1, pair), F32)]
    current = lrecv[0].astype(F32)
    for j in range(NY):
        before.append(before[-1] + trecv[j][0:1, :])
        if j:
            qbuf[j - 1] = current
            current = jnp.exp(trecv[j][0:1, :]) * current + lrecv[j].astype(F32)
    size = STATE // NZ
    for k in range(NZ):
        rsend[k] = current[k * size : (k + 1) * size, :].astype(BF16)
    dsend[...] = jnp.broadcast_to(before[NY], (8, pair))
    for k in range(1, NZ):
        to = (z + k) % NZ
        send(rsend.at[to], rrecv.at[z], r_ss, r_rs, device(dz=k))
        send(dsend.at[pl.ds(0, 1), :], drecv.at[z, pl.ds(0, 1), :], d_ss, d_rs, device(dz=k))
    rrecv[z] = rsend[z]
    drecv[z] = dsend[...]
    relay(5)

    arrived(rrecv.at[pl.ds(0, NZ - 1)], r_rs)
    arrived(drecv.at[pl.ds(0, NZ - 1), pl.ds(0, 1), :], d_rs)
    current = jnp.zeros((size, pair), F32)
    for k in range(NZ):
        esend[k] = current.astype(BF16)
        current = jnp.exp(drecv[k][0:1, :]) * current + rrecv[k].astype(F32)
    for k in range(1, NZ):
        to = (z + k) % NZ
        send(esend.at[to], erecv.at[z], e_ss, e_rs, device(dz=k))
    erecv[z] = esend[z]
    relay(8)
    arrived(erecv.at[pl.ds(0, NZ - 1)], e_rs)
    entry = jnp.concatenate([erecv[k].astype(F32) for k in range(NZ)], axis=0)
    ssend[0] = entry.astype(BF16)
    for j in range(1, NY):
        ssend[j] = (qbuf[j - 1] + jnp.exp(before[j]) * entry).astype(BF16)
    for k in range(1, NY):
        to = (y + k) % NY
        send(ssend.at[to], srecv.at[y], s_ss, s_rs, device(dy=k))
    srecv[y] = ssend[y]
    relay(11)
    arrived(srecv.at[pl.ds(0, NY - 1)], s_rs)

    grown = jnp.exp(cum)
    squares = jnp.zeros((tokens, WIDTH), F32)
    for j in range(NY):
        inter = dot(cmat, srecv[j])
        for i in range(heads // NY):
            h = j * heads // NY + i
            span = slice(h * WIDTH, (h + 1) * WIDTH)
            value = ybuf[:, span] + grown[:, h : h + 1] * inter[:, i * WIDTH : (i + 1) * WIDTH]
            value = value * smbuf[:, span]
            ybuf[:, span] = value
            squares = squares + value * value
    mean = jnp.sum(squares, axis=1, keepdims=True) * (1.0 / channels)
    scale = lax.rsqrt(mean + 1e-05)
    abuf[0] = (ybuf[...] * scale * gain_ref[...]).astype(BF16)

    turns = (0, -1, 1, 2)

    def a_part(turn, half):
        return abuf.at[turn, pl.ds(half * thalf, thalf), :]

    for i in range(2):
        for d, sign in enumerate((1, -1)):
            half = i if d == 0 else 1 - i
            send(
                a_part(0, half),
                a_part(1 + d, half),
                a_ss,
                a_rs.at[d, i],
                device(dy=sign),
            )

    distances = (0, 1, -1, 2, -2, 3, -3, 4)
    stages = ((0, 1), (1, 3), (3, 4))
    whole = (0, NY)

    def owner(n):
        origin = (z + distances[n]) % NZ
        return origin // NC, origin % NC

    def lanes_of(half):
        return pl.ds(0, cols) if half is None else pl.ds(half * chalf, chalf)

    def index_of(span, half):
        return (half or 0) if span == whole else stages.index(span)

    def partner_copy(n, span, half):
        rows = pl.ds(span[0], span[1] - span[0])
        index = index_of(span, half)
        return (
            part_sums.at[1 - core, n, rows, :, lanes_of(half)],
            precv.at[n, rows, :, lanes_of(half)],
            p_ss,
            p_rs.at[n, index],
        )

    def multiply(n, span, half):
        origin = (z + distances[n]) % NZ
        if half is None:
            part = jnp.concatenate([wall[origin, 0], wall[origin, 1]], axis=1)
        else:
            part = wall[origin, half]
        width = part.shape[1]
        step = min(2, span[1] - span[0])
        for first in range(span[0], span[1], step):
            a = abuf[first : first + step].reshape(step * tokens, channels)
            total = dot(a, part).reshape(step, tokens, width)
            for c in range(NC):
                part_sums[c, n, first : first + step, :, lanes_of(half)] = total[
                    :, c * share : (c + 1) * share, :
                ]
        send(*partner_copy(n, span, half), device(dc=1))

    slab = share // NX

    def chip_sum(n, span, half):
        _, dst, _, rs = partner_copy(n, span, half)
        arrived(dst, rs)
        lanes = lanes_of(half)
        both = part_sums[core, n, span[0] : span[1], :, lanes]
        both = both + precv[n, span[0] : span[1], :, lanes]
        for j in range(NX):

            @pl.when(x == j)
            def _():
                xown[n, span[0] : span[1], :, lanes] = both[:, j * slab : (j + 1) * slab, :]

        both = both.astype(BF16)
        for j in range(NX):
            xsend[n, j, span[0] : span[1], :, lanes] = both[:, j * slab : (j + 1) * slab, :]
        rows = pl.ds(span[0], span[1] - span[0])
        for k in range(1, NX):
            send(
                xsend.at[n, (x + k) % NX, rows, :, lanes],
                xrecv.at[n, k - 1, rows, :, lanes],
                x_ss,
                x_rs.at[n],
                device(dx=k),
            )

    mine = pl.ds(pl.multiple_of(y * cols, cols), cols)
    place = pl.ds(pl.multiple_of(core * share + x * slab, slab), slab)

    def finish(n):
        value = xown[n]
        arrived(xrecv.at[n], x_rs.at[n])
        for k in range(1, NX):
            value = value + xrecv[n, k - 1].astype(F32)
        fsend[n] = value.astype(BF16)
        to_x, to_core = owner(n)
        for t in (3, 1, 2):
            to = (z * NY + (y + turns[t]) % NY, to_x * NC + to_core)
            send(fsend.at[n, t], out_ref.at[place, mine], f_ss, f_rs, to)
        own = (to_x == x) & (to_core == core)

        @pl.when(own)
        def _():
            pltpu.make_async_copy(fsend.at[n, 0], out_ref.at[place, mine], f_rs).start()

        @pl.when(jnp.logical_not(own))
        def _():
            send(
                fsend.at[n, 0], out_ref.at[place, mine], o_ss, f_rs, (seq, to_x * NC + to_core)
            )

    pending = []

    def unit(n, span, half=None):
        multiply(n, span, half)
        pending.append((n, span, half))
        if len(pending) > 1:
            chip_sum(*pending.pop(0))

    relay(11)
    for n in range(3):
        unit(n, stages[0])
    relay(12)
    for d, sign in enumerate((1, -1)):
        arrived(a_part(1 + d, d), a_rs.at[d, 0])
        send(a_part(1 + d, d), a_part(3, d), a_ss, a_rs.at[d, 2], device(dy=sign))
    relay(13)
    for n in range(3, 5):
        unit(n, stages[0])
    for d in range(2):
        arrived(a_part(1 + d, 1 - d), a_rs.at[d, 1])
    for n in range(5):
        unit(n, stages[1])
    relay(15)
    sent(lsend.at[pl.ds(0, NY - 1)], l_ss)
    sent(tsend.at[pl.ds(0, NY - 1), pl.ds(0, 1), :], t_ss)
    sent(rsend.at[pl.ds(0, NZ - 1)], r_ss)
    sent(drecv.at[pl.ds(0, NZ - 1), pl.ds(0, 1), :], d_ss)
    sent(esend.at[pl.ds(0, NZ - 1)], e_ss)
    sent(ssend.at[pl.ds(0, NY - 1)], s_ss)
    for d in range(2):
        arrived(a_part(3, d), a_rs.at[d, 2])
    for n in range(5):
        unit(n, stages[2])
    relay(16)
    unit(5, whole)
    unit(6, whole)
    sent(abuf.at[pl.ds(0, 3)], a_ss)
    relay(17)
    unit(7, whole, 0)
    relay(18)
    unit(7, whole, 1)
    chip_sum(*pending.pop(0))
    for n in range(NZ - 1):
        finish(n)
    finish(NZ - 1)

    sent(wall.at[pl.ds(0, NZ - 1)], w_ss)
    sent(precv, p_ss)
    sent(xrecv, x_ss)
    arrived(out_ref, f_rs)
    sent(fsend.at[:, pl.ds(1, NY - 1)], f_ss)
    sent(fsend.at[pl.ds(0, NZ - 1), 0], o_ss)


def shards(
    x_in, multiplier_channels, b_proj, c_proj, dt_raw, dt_bias, a_log, skip_d, norm_gain, w_out
):
    tokens, channels = x_in.shape
    depth, cols = w_out.shape
    pair = channels // NY
    size = STATE // NZ
    vmem = pl.BlockSpec(memory_space=pltpu.VMEM)
    dma = pltpu.SemaphoreType.DMA
    half = cols // 2
    share = tokens // NC
    heads = channels // WIDTH
    scratch = [
        pltpu.VMEM((heads, tokens), F32),
        pltpu.VMEM((1, heads), F32),
        pltpu.VMEM((1, heads), F32),
        pltpu.VMEM((1, heads), F32),
        pltpu.VMEM((1, channels), F32),
        pltpu.VMEM((tokens, STATE), BF16),
        pltpu.VMEM((tokens, STATE), BF16),
        pltpu.VMEM((tokens, channels), BF16),
        pltpu.VMEM((tokens, channels), BF16),
        pltpu.VMEM((NZ, 2, depth, half), BF16),
        pltpu.VMEM((NY, tokens, channels), BF16),
        pltpu.VMEM((tokens, channels), F32),
        pltpu.VMEM((tokens, channels), F32),
        pltpu.VMEM((NY - 1, STATE, pair), F32),
        pltpu.VMEM((NY, STATE, pair), BF16),
        pltpu.VMEM((NY, STATE, pair), BF16),
        pltpu.VMEM((NY, 8, pair), F32),
        pltpu.VMEM((NY, 8, pair), F32),
        pltpu.VMEM((NZ, size, pair), BF16),
        pltpu.VMEM((NZ, size, pair), BF16),
        pltpu.VMEM((8, pair), F32),
        pltpu.VMEM((NZ, 8, pair), F32),
        pltpu.VMEM((NZ, size, pair), BF16),
        pltpu.VMEM((NZ, size, pair), BF16),
        pltpu.VMEM((NY, STATE, pair), BF16),
        pltpu.VMEM((NY, STATE, pair), BF16),
        pltpu.VMEM((NC, NZ, NY, share, cols), F32),
        pltpu.VMEM((NZ, NY, share, cols), F32),
        pltpu.VMEM((NZ, NX, NY, share // NX, cols), BF16),
        pltpu.VMEM((NZ, NY, share // NX, cols), F32),
        pltpu.VMEM((NZ, NX - 1, NY, share // NX, cols), BF16),
        pltpu.VMEM((NZ, NY, share // NX, cols), BF16),
        dma((9,)),
        dma((2,)),
        dma, dma((2, 4, 4)),
        dma, dma, dma, dma,
        dma, dma, dma, dma,
        dma, dma,
        dma, dma,
        dma, dma((2, 3)),
        dma, dma((NZ, 3)),
        dma, dma((NZ,)),
        dma, dma, dma,
    ]
    return pl.pallas_call(
        kernel,
        out_shape=pltpu.VMEM((tokens, channels), BF16),
        in_specs=[pl.BlockSpec(memory_space=pl.ANY)] * 10,
        out_specs=vmem,
        scratch_shapes=scratch,
        compiler_params=pltpu.CompilerParams(
            collective_id=0, has_side_effects=True, vmem_limit_bytes=56 * 1024 * 1024
        ),
        name="mixer",
    )(
        dt_raw.T,
        dt_bias.reshape(1, -1),
        a_log.reshape(1, -1),
        skip_d.reshape(1, -1),
        norm_gain.reshape(1, -1),
        b_proj,
        c_proj,
        x_in,
        multiplier_channels,
        w_out,
    )


def solution(mesh):
    return jax.shard_map(
        shards,
        mesh=mesh,
        in_specs=(
            P("seq", "grp"),
            P("seq", "grp"),
            P("seq", "grp"),
            P("seq", "grp"),
            P("seq", "grp"),
            P("grp"),
            P("grp"),
            P("grp"),
            P("grp"),
            P("grp", "seq"),
        ),
        out_specs=P("seq", "grp"),
        check_vma=False,
    )
```

```python
import jax
import jax.numpy as jnp
from jax import lax
from jax.experimental import pallas as pl
from jax.experimental.pallas import tpu as pltpu
from jax.sharding import PartitionSpec as P

MESH = pl.DeviceIdType.MESH
HIGH = lax.Precision.HIGHEST
WIDTH = 128
STATE = 128
NZ, NY, NX, NC = 8, 4, 4, 2
F32 = jnp.float32
BF16 = jnp.bfloat16


def split(value):
    high = value.astype(BF16)
    return high, (value - high.astype(F32)).astype(BF16)


def dot(a, b, dims=((1,), (0,))):
    return lax.dot_general(a, b, (dims, ((), ())), preferred_element_type=F32)


def kernel(
    dt_hbm, bias_hbm, alog_hbm, skip_hbm, gain_hbm, b_hbm, c_hbm, x_hbm, m_hbm, w_ref,
    out_ref,
    dt_ref, bias_ref, alog_ref, skip_ref, gain_ref, b_ref, c_ref, x_ref, m_ref, wall, abuf, ybuf, smbuf, qbuf,
    lsend, lrecv, tsend, trecv,
    rsend, rrecv, dsend, drecv,
    esend, erecv, ssend, srecv,
    part_sums, precv, xsend, xown, xrecv, fsend,
    in_sems, w_local, w_ss, w_rs, l_ss, l_rs, t_ss, t_rs, r_ss, r_rs, d_ss, d_rs,
    e_ss, e_rs, s_ss, s_rs, a_ss, a_rs, p_ss, p_rs, x_ss, x_rs, f_ss, o_ss, f_rs,
):
    seq, grp = lax.axis_index("seq"), lax.axis_index("grp")
    z, y = seq // NY, seq % NY
    x, core = grp // NC, grp % NC
    tokens, channels = x_ref.shape
    heads = channels // WIDTH
    pair = channels // NY
    cols = w_ref.shape[1]
    khalf = w_ref.shape[0] // 2
    chalf = cols // 2
    thalf = tokens // 2
    share = tokens // NC

    def device(dz=0, dy=0, dx=0, dc=0):
        return (
            ((z + dz) % NZ) * NY + (y + dy) % NY,
            ((x + dx) % NX) * NC + (core + dc) % NC,
        )

    def remote(src, dst, ss, rs, to):
        return pltpu.make_async_remote_copy(
            src_ref=src, dst_ref=dst, send_sem=ss, recv_sem=rs, device_id=to, device_id_type=MESH
        )

    def send(src, dst, ss, rs, to):
        remote(src, dst, ss, rs, to).start()

    def sent(like, ss):
        remote(like, like, ss, f_rs, device(dz=1)).wait_send()

    def arrived(like, rs):
        remote(like, like, w_ss, rs, device(dz=1)).wait_recv()

    barrier = pltpu.get_barrier_semaphore()
    others = (
        [dict(dz=k) for k in range(1, NZ)]
        + [dict(dy=k) for k in range(1, NY)]
        + [dict(dx=k, dc=c) for k in range(NX) for c in range(NC) if k or c]
    )
    for other in others:
        pl.semaphore_signal(barrier, inc=1, device_id=device(**other), device_id_type=MESH)
    own_w = []
    for i in range(2):
        copy = pltpu.make_async_copy(
            w_ref.at[:, i * chalf : (i + 1) * chalf], wall.at[z, i], w_local.at[i]
        )
        copy.start()
        own_w.append(copy)
    loads = [
        pltpu.make_async_copy(src, dst, in_sems.at[i])
        for i, (src, dst) in enumerate(
            (
                (dt_hbm, dt_ref),
                (bias_hbm, bias_ref),
                (alog_hbm, alog_ref),
                (x_hbm, x_ref),
                (b_hbm, b_ref),
                (c_hbm, c_ref),
                (skip_hbm, skip_ref),
                (m_hbm, m_ref),
                (gain_hbm, gain_ref),
            )
        )
    ]
    for copy in loads:
        copy.start()

    pl.semaphore_wait(barrier, len(others))

    def w_part(origin, d, i):
        half = i % 2 if d == 0 else 1 - i % 2
        return wall.at[origin, i // 2, pl.ds(half * khalf, khalf), :]

    last = NZ // 2
    items = [(step, i) for step in range(last) for i in range(4)] + [(last, 0), (last, 2)]
    done = [0]

    def place_of(step, i):
        return 4 * step + (i if step < last - 1 else i // 2)

    def relay(count):
        while done[0] < count:
            step, i = items[done[0]]
            done[0] += 1
            for d, sign in enumerate((1, -1)):
                part = source = w_part((z - sign * step) % NZ, d, i)
                if not step:
                    half = i % 2 if d == 0 else 1 - i % 2
                    source = w_ref.at[
                        pl.ds(half * khalf, khalf), pl.ds(i // 2 * chalf, chalf)
                    ]
                else:
                    arrived(part, w_rs.at[d, place_of(step - 1, i)])
                if step < last - 1 or (step == last - 1 and i % 2 == 0):
                    send(source, part, w_ss, w_rs.at[d, place_of(step, i)], device(dz=sign))

    relay(3)

    for copy in loads + own_w:
        copy.wait()
    raw = jnp.transpose(dt_ref[...]) + bias_ref[...]
    dt = jnp.maximum(raw, 0.0) + jnp.log1p(jnp.exp(-jnp.abs(raw)))
    la = -jnp.exp(alog_ref[...]) * dt
    rows = lax.broadcasted_iota(jnp.int32, (tokens, tokens), 0)
    columns = lax.broadcasted_iota(jnp.int32, (tokens, tokens), 1)
    mask = rows >= columns
    cum = lax.dot_general(
        mask.astype(F32), la, (((1,), (0,)), ((), ())), precision=HIGH, preferred_element_type=F32
    )
    total = cum[tokens - 1 : tokens, :]
    weight = jnp.exp(total - cum) * dt

    bmat, cmat = b_ref[...], c_ref[...]
    for j in range(NY):
        parts = []
        for h in range(j * heads // NY, (j + 1) * heads // NY):
            xh = x_ref[:, h * WIDTH : (h + 1) * WIDTH].astype(F32)
            parts.append(xh * weight[:, h : h + 1])
        high, low = split(jnp.concatenate(parts, axis=1))
        state = dot(bmat, high, ((0,), (0,))) + dot(bmat, low, ((0,), (0,)))
        lsend[j] = state.astype(BF16)
        tsend[j] = jnp.concatenate(
            [
                jnp.broadcast_to(total[:, h : h + 1], (8, WIDTH))
                for h in range(j * heads // NY, (j + 1) * heads // NY)
            ],
            axis=1,
        )
    for k in range(1, NY):
        to = (y + k) % NY
        send(lsend.at[to], lrecv.at[y], l_ss, l_rs, device(dy=k))
        send(tsend.at[to, pl.ds(0, 1), :], trecv.at[y, pl.ds(0, 1), :], t_ss, t_rs, device(dy=k))
    lrecv[y] = lsend[y]
    trecv[y] = tsend[y]

    logits = dot(cmat, bmat, ((1,), (1,)))
    cum_t = jnp.transpose(cum)
    dt_t = jnp.transpose(dt)
    for h in range(heads):
        span = slice(h * WIDTH, (h + 1) * WIDTH)
        decay = jnp.exp(jnp.where(mask, cum[:, h : h + 1] - cum_t[h : h + 1, :], -1e30))
        high, low = split(decay * logits * dt_t[h : h + 1, :])
        xh = x_ref[:, span]
        ybuf[:, span] = dot(high, xh) + dot(low, xh) + skip_ref[:, h : h + 1] * xh.astype(F32)
        gate = m_ref[:, span].astype(F32)
        smbuf[:, span] = gate / (1.0 + jnp.exp(-gate))

    arrived(lrecv.at[pl.ds(0, NY - 1)], l_rs)
    arrived(trecv.at[pl.ds(0, NY - 1), pl.ds(0, 1), :], t_rs)
    before = [jnp.zeros((1, pair), F32)]
    current = lrecv[0].astype(F32)
    for j in range(NY):
        before.append(before[-1] + trecv[j][0:1, :])
        if j:
            qbuf[j - 1] = current
            current = jnp.exp(trecv[j][0:1, :]) * current + lrecv[j].astype(F32)
    size = STATE // NZ
    for k in range(NZ):
        rsend[k] = current[k * size : (k + 1) * size, :].astype(BF16)
    dsend[...] = jnp.broadcast_to(before[NY], (8, pair))
    for k in range(1, NZ):
        to = (z + k) % NZ
        send(rsend.at[to], rrecv.at[z], r_ss, r_rs, device(dz=k))
        send(dsend.at[pl.ds(0, 1), :], drecv.at[z, pl.ds(0, 1), :], d_ss, d_rs, device(dz=k))
    rrecv[z] = rsend[z]
    drecv[z] = dsend[...]
    relay(5)

    arrived(rrecv.at[pl.ds(0, NZ - 1)], r_rs)
    arrived(drecv.at[pl.ds(0, NZ - 1), pl.ds(0, 1), :], d_rs)
    current = jnp.zeros((size, pair), F32)
    for k in range(NZ):
        esend[k] = current.astype(BF16)
        current = jnp.exp(drecv[k][0:1, :]) * current + rrecv[k].astype(F32)
    for k in range(1, NZ):
        to = (z + k) % NZ
        send(esend.at[to], erecv.at[z], e_ss, e_rs, device(dz=k))
    erecv[z] = esend[z]
    relay(8)
    arrived(erecv.at[pl.ds(0, NZ - 1)], e_rs)
    entry = jnp.concatenate([erecv[k].astype(F32) for k in range(NZ)], axis=0)
    ssend[0] = entry.astype(BF16)
    for j in range(1, NY):
        ssend[j] = (qbuf[j - 1] + jnp.exp(before[j]) * entry).astype(BF16)
    for k in range(1, NY):
        to = (y + k) % NY
        send(ssend.at[to], srecv.at[y], s_ss, s_rs, device(dy=k))
    srecv[y] = ssend[y]
    relay(11)
    arrived(srecv.at[pl.ds(0, NY - 1)], s_rs)

    grown = jnp.exp(cum)
    squares = jnp.zeros((tokens, WIDTH), F32)
    for j in range(NY):
        inter = dot(cmat, srecv[j])
        for i in range(heads // NY):
            h = j * heads // NY + i
            span = slice(h * WIDTH, (h + 1) * WIDTH)
            value = ybuf[:, span] + grown[:, h : h + 1] * inter[:, i * WIDTH : (i + 1) * WIDTH]
            value = value * smbuf[:, span]
            ybuf[:, span] = value
            squares = squares + value * value
    mean = jnp.sum(squares, axis=1, keepdims=True) * (1.0 / channels)
    scale = lax.rsqrt(mean + 1e-05)
    abuf[0] = (ybuf[...] * scale * gain_ref[...]).astype(BF16)

    turns = (0, -1, 1, 2)

    def a_part(turn, half):
        return abuf.at[turn, pl.ds(half * thalf, thalf), :]

    for i in range(2):
        for d, sign in enumerate((1, -1)):
            half = i if d == 0 else 1 - i
            send(
                a_part(0, half),
                a_part(1 + d, half),
                a_ss,
                a_rs.at[d, i],
                device(dy=sign),
            )

    distances = (0, 1, -1, 2, -2, 3, -3, 4)
    stages = ((0, 1), (1, 3), (3, 4))
    whole = (0, NY)

    def owner(n):
        origin = (z + distances[n]) % NZ
        return origin // NC, origin % NC

    def lanes_of(half):
        return pl.ds(0, cols) if half is None else pl.ds(half * chalf, chalf)

    def index_of(span, half):
        return (half or 0) if span == whole else stages.index(span)

    def partner_copy(n, span, half):
        rows = pl.ds(span[0], span[1] - span[0])
        index = index_of(span, half)
        return (
            part_sums.at[1 - core, n, rows, :, lanes_of(half)],
            precv.at[n, rows, :, lanes_of(half)],
            p_ss,
            p_rs.at[3 * n + index if n < 5 else 10 + n + index],
        )

    def multiply(n, span, half):
        origin = (z + distances[n]) % NZ
        if half is None:
            part = jnp.concatenate([wall[origin, 0], wall[origin, 1]], axis=1)
        else:
            part = wall[origin, half]
        width = part.shape[1]
        step = min(2, span[1] - span[0])
        for first in range(span[0], span[1], step):
            a = abuf[first : first + step].reshape(step * tokens, channels)
            total = dot(a, part).reshape(step, tokens, width)
            for c in range(NC):
                part_sums[c, n, first : first + step, :, lanes_of(half)] = total[
                    :, c * share : (c + 1) * share, :
                ]
        send(*partner_copy(n, span, half), device(dc=1))

    slab = share // NX

    def chip_sum(n, span, half):
        _, dst, _, rs = partner_copy(n, span, half)
        arrived(dst, rs)
        lanes = lanes_of(half)
        both = part_sums[core, n, span[0] : span[1], :, lanes]
        both = both + precv[n, span[0] : span[1], :, lanes]
        for j in range(NX):

            @pl.when(x == j)
            def _():
                xown[n, span[0] : span[1], :, lanes] = both[:, j * slab : (j + 1) * slab, :]

        both = both.astype(BF16)
        for j in range(NX):
            xsend[n, j, span[0] : span[1], :, lanes] = both[:, j * slab : (j + 1) * slab, :]
        rows = pl.ds(span[0], span[1] - span[0])
        for k in range(1, NX):
            send(
                xsend.at[n, (x + k) % NX, rows, :, lanes],
                xrecv.at[n, k - 1, rows, :, lanes],
                x_ss,
                x_rs.at[n],
                device(dx=k),
            )

    mine = pl.ds(pl.multiple_of(y * cols, cols), cols)
    place = pl.ds(pl.multiple_of(core * share + x * slab, slab), slab)

    def finish(n):
        value = xown[n]
        arrived(xrecv.at[n], x_rs.at[n])
        for k in range(1, NX):
            value = value + xrecv[n, k - 1].astype(F32)
        fsend[n] = value.astype(BF16)
        to_x, to_core = owner(n)
        for t in (3, 1, 2):
            to = (z * NY + (y + turns[t]) % NY, to_x * NC + to_core)
            send(fsend.at[n, t], out_ref.at[place, mine], f_ss, f_rs, to)
        own = (to_x == x) & (to_core == core)

        @pl.when(own)
        def _():
            pltpu.make_async_copy(fsend.at[n, 0], out_ref.at[place, mine], f_rs).start()

        @pl.when(jnp.logical_not(own))
        def _():
            send(
                fsend.at[n, 0], out_ref.at[place, mine], o_ss, f_rs, (seq, to_x * NC + to_core)
            )

    pending = []

    def unit(n, span, half=None):
        multiply(n, span, half)
        pending.append((n, span, half))
        if len(pending) > 1:
            chip_sum(*pending.pop(0))

    relay(11)
    for n in range(3):
        unit(n, stages[0])
    relay(12)
    for d, sign in enumerate((1, -1)):
        arrived(a_part(1 + d, d), a_rs.at[d, 0])
        send(a_part(1 + d, d), a_part(3, d), a_ss, a_rs.at[d, 2], device(dy=sign))
    relay(13)
    for n in range(3, 5):
        unit(n, stages[0])
    for d in range(2):
        arrived(a_part(1 + d, 1 - d), a_rs.at[d, 1])
    for n in range(5):
        unit(n, stages[1])
    relay(15)
    sent(lsend.at[pl.ds(0, NY - 1)], l_ss)
    sent(tsend.at[pl.ds(0, NY - 1), pl.ds(0, 1), :], t_ss)
    sent(rsend.at[pl.ds(0, NZ - 1)], r_ss)
    sent(drecv.at[pl.ds(0, NZ - 1), pl.ds(0, 1), :], d_ss)
    sent(esend.at[pl.ds(0, NZ - 1)], e_ss)
    sent(ssend.at[pl.ds(0, NY - 1)], s_ss)
    for d in range(2):
        arrived(a_part(3, d), a_rs.at[d, 2])
    for n in range(5):
        unit(n, stages[2])
    relay(16)
    unit(5, whole)
    unit(6, whole)
    sent(abuf.at[pl.ds(0, 3)], a_ss)
    relay(17)
    unit(7, whole, 0)
    relay(18)
    unit(7, whole, 1)
    chip_sum(*pending.pop(0))
    for n in range(NZ - 1):
        finish(n)
    finish(NZ - 1)

    sent(wall.at[pl.ds(0, NZ - 1)], w_ss)
    sent(precv, p_ss)
    sent(xrecv, x_ss)
    arrived(out_ref, f_rs)
    sent(fsend.at[:, pl.ds(1, NY - 1)], f_ss)
    sent(fsend.at[pl.ds(0, NZ - 1), 0], o_ss)


def shards(
    x_in, multiplier_channels, b_proj, c_proj, dt_raw, dt_bias, a_log, skip_d, norm_gain, w_out
):
    tokens, channels = x_in.shape
    depth, cols = w_out.shape
    pair = channels // NY
    size = STATE // NZ
    vmem = pl.BlockSpec(memory_space=pltpu.VMEM)
    dma = pltpu.SemaphoreType.DMA
    half = cols // 2
    share = tokens // NC
    heads = channels // WIDTH
    scratch = [
        pltpu.VMEM((heads, tokens), F32),
        pltpu.VMEM((1, heads), F32),
        pltpu.VMEM((1, heads), F32),
        pltpu.VMEM((1, heads), F32),
        pltpu.VMEM((1, channels), F32),
        pltpu.VMEM((tokens, STATE), BF16),
        pltpu.VMEM((tokens, STATE), BF16),
        pltpu.VMEM((tokens, channels), BF16),
        pltpu.VMEM((tokens, channels), BF16),
        pltpu.VMEM((NZ, 2, depth, half), BF16),
        pltpu.VMEM((NY, tokens, channels), BF16),
        pltpu.VMEM((tokens, channels), F32),
        pltpu.VMEM((tokens, channels), F32),
        pltpu.VMEM((NY - 1, STATE, pair), F32),
        pltpu.VMEM((NY, STATE, pair), BF16),
        pltpu.VMEM((NY, STATE, pair), BF16),
        pltpu.VMEM((NY, 8, pair), F32),
        pltpu.VMEM((NY, 8, pair), F32),
        pltpu.VMEM((NZ, size, pair), BF16),
        pltpu.VMEM((NZ, size, pair), BF16),
        pltpu.VMEM((8, pair), F32),
        pltpu.VMEM((NZ, 8, pair), F32),
        pltpu.VMEM((NZ, size, pair), BF16),
        pltpu.VMEM((NZ, size, pair), BF16),
        pltpu.VMEM((NY, STATE, pair), BF16),
        pltpu.VMEM((NY, STATE, pair), BF16),
        pltpu.VMEM((NC, NZ, NY, share, cols), F32),
        pltpu.VMEM((NZ, NY, share, cols), F32),
        pltpu.VMEM((NZ, NX, NY, share // NX, cols), BF16),
        pltpu.VMEM((NZ, NY, share // NX, cols), F32),
        pltpu.VMEM((NZ, NX - 1, NY, share // NX, cols), BF16),
        pltpu.VMEM((NZ, NY, share // NX, cols), BF16),
        dma((9,)),
        dma((2,)),
        dma, dma((2, 14)),
        dma, dma, dma, dma,
        dma, dma, dma, dma,
        dma, dma,
        dma, dma,
        dma, dma((2, 3)),
        dma, dma((19,)),
        dma, dma((NZ,)),
        dma, dma, dma,
    ]
    return pl.pallas_call(
        kernel,
        out_shape=pltpu.VMEM((tokens, channels), BF16),
        in_specs=[pl.BlockSpec(memory_space=pl.ANY)] * 10,
        out_specs=vmem,
        scratch_shapes=scratch,
        compiler_params=pltpu.CompilerParams(
            collective_id=0, has_side_effects=True, vmem_limit_bytes=56 * 1024 * 1024
        ),
        name="mixer",
    )(
        dt_raw.T,
        dt_bias.reshape(1, -1),
        a_log.reshape(1, -1),
        skip_d.reshape(1, -1),
        norm_gain.reshape(1, -1),
        b_proj,
        c_proj,
        x_in,
        multiplier_channels,
        w_out,
    )


def solution(mesh):
    return jax.shard_map(
        shards,
        mesh=mesh,
        in_specs=(
            P("seq", "grp"),
            P("seq", "grp"),
            P("seq", "grp"),
            P("seq", "grp"),
            P("seq", "grp"),
            P("grp"),
            P("grp"),
            P("grp"),
            P("grp"),
            P("grp", "seq"),
        ),
        out_specs=P("seq", "grp"),
        check_vma=False,
    )
```

```python
import jax
import jax.numpy as jnp
from jax import lax
from jax.experimental import pallas as pl
from jax.experimental.pallas import tpu as pltpu
from jax.sharding import PartitionSpec as P

MESH = pl.DeviceIdType.MESH
HIGH = lax.Precision.HIGHEST
WIDTH = 128
STATE = 128
NZ, NY, NX, NC = 8, 4, 4, 2
F32 = jnp.float32
BF16 = jnp.bfloat16


def split(value):
    high = value.astype(BF16)
    return high, (value - high.astype(F32)).astype(BF16)


def dot(a, b, dims=((1,), (0,))):
    return lax.dot_general(a, b, (dims, ((), ())), preferred_element_type=F32)


def kernel(
    dt_hbm, bias_hbm, alog_hbm, skip_hbm, gain_hbm, b_hbm, c_hbm, x_hbm, m_hbm, w_ref,
    out_ref,
    dt_ref, bias_ref, alog_ref, skip_ref, gain_ref, b_ref, c_ref, x_ref, m_ref, wall, abuf, ybuf, smbuf, qbuf,
    lsend, lrecv, tsend, trecv,
    rsend, rrecv, dsend, drecv,
    esend, erecv, ssend, srecv,
    part_sums, precv, xsend, xown, xrecv, fsend,
    in_sems, w_local, w_ss, w_rs, l_ss, l_rs, t_ss, t_rs, r_ss, r_rs, d_ss, d_rs,
    e_ss, e_rs, s_ss, s_rs, a_ss, a_rs, p_ss, p_rs, x_ss, x_rs, f_ss, o_ss, f_rs,
):
    seq, grp = lax.axis_index("seq"), lax.axis_index("grp")
    z, y = seq // NY, seq % NY
    x, core = grp // NC, grp % NC
    tokens, channels = x_ref.shape
    heads = channels // WIDTH
    pair = channels // NY
    cols = w_ref.shape[1]
    khalf = w_ref.shape[0] // 2
    chalf = cols // 2
    thalf = tokens // 2
    share = tokens // NC

    def device(dz=0, dy=0, dx=0, dc=0):
        return (
            ((z + dz) % NZ) * NY + (y + dy) % NY,
            ((x + dx) % NX) * NC + (core + dc) % NC,
        )

    def remote(src, dst, ss, rs, to):
        return pltpu.make_async_remote_copy(
            src_ref=src, dst_ref=dst, send_sem=ss, recv_sem=rs, device_id=to, device_id_type=MESH
        )

    def send(src, dst, ss, rs, to):
        remote(src, dst, ss, rs, to).start()

    def sent(like, ss):
        remote(like, like, ss, f_rs, device(dz=1)).wait_send()

    def arrived(like, rs):
        remote(like, like, w_ss, rs, device(dz=1)).wait_recv()

    barrier = pltpu.get_barrier_semaphore()
    others = (
        [dict(dz=k) for k in range(1, NZ)]
        + [dict(dy=k) for k in range(1, NY)]
        + [dict(dx=k, dc=c) for k in range(NX) for c in range(NC) if k or c]
    )
    for other in others:
        pl.semaphore_signal(barrier, inc=1, device_id=device(**other), device_id_type=MESH)
    own_w = []
    for i in range(2):
        copy = pltpu.make_async_copy(
            w_ref.at[:, i * chalf : (i + 1) * chalf], wall.at[z, i], w_local.at[i]
        )
        copy.start()
        own_w.append(copy)
    loads = [
        pltpu.make_async_copy(src, dst, in_sems.at[i])
        for i, (src, dst) in enumerate(
            (
                (dt_hbm, dt_ref),
                (bias_hbm, bias_ref),
                (alog_hbm, alog_ref),
                (x_hbm, x_ref),
                (b_hbm, b_ref),
                (c_hbm, c_ref),
                (skip_hbm, skip_ref),
                (m_hbm, m_ref),
                (gain_hbm, gain_ref),
            )
        )
    ]
    for copy in loads:
        copy.start()

    pl.semaphore_wait(barrier, len(others))

    def w_part(origin, d, i):
        half = i % 2 if d == 0 else 1 - i % 2
        return wall.at[origin, i // 2, pl.ds(half * khalf, khalf), :]

    last = NZ // 2
    items = [(step, i) for step in range(last) for i in range(4)] + [(last, 0), (last, 2)]
    done = [0]

    def place_of(step, i):
        return 4 * step + (i if step < last - 1 else i // 2)

    def relay(count):
        while done[0] < count:
            step, i = items[done[0]]
            done[0] += 1
            for d, sign in enumerate((1, -1)):
                part = source = w_part((z - sign * step) % NZ, d, i)
                if not step:
                    half = i % 2 if d == 0 else 1 - i % 2
                    source = w_ref.at[
                        pl.ds(half * khalf, khalf), pl.ds(i // 2 * chalf, chalf)
                    ]
                else:
                    arrived(part, w_rs.at[d, place_of(step - 1, i)])
                if step < last - 1 or (step == last - 1 and i % 2 == 0):
                    send(source, part, w_ss, w_rs.at[d, place_of(step, i)], device(dz=sign))

    relay(3)

    for copy in loads + own_w:
        copy.wait()
    raw = jnp.transpose(dt_ref[...]) + bias_ref[...]
    dt = jnp.maximum(raw, 0.0) + jnp.log1p(jnp.exp(-jnp.abs(raw)))
    la = -jnp.exp(alog_ref[...]) * dt
    rows = lax.broadcasted_iota(jnp.int32, (tokens, tokens), 0)
    columns = lax.broadcasted_iota(jnp.int32, (tokens, tokens), 1)
    mask = rows >= columns
    cum = lax.dot_general(
        mask.astype(F32), la, (((1,), (0,)), ((), ())), precision=HIGH, preferred_element_type=F32
    )
    total = cum[tokens - 1 : tokens, :]
    weight = jnp.exp(total - cum) * dt

    bmat, cmat = b_ref[...], c_ref[...]
    for j in range(NY):
        parts = []
        for h in range(j * heads // NY, (j + 1) * heads // NY):
            xh = x_ref[:, h * WIDTH : (h + 1) * WIDTH].astype(F32)
            parts.append(xh * weight[:, h : h + 1])
        high, low = split(jnp.concatenate(parts, axis=1))
        state = dot(bmat, high, ((0,), (0,))) + dot(bmat, low, ((0,), (0,)))
        lsend[j] = state.astype(BF16)
        tsend[j] = jnp.concatenate(
            [
                jnp.broadcast_to(total[:, h : h + 1], (8, WIDTH))
                for h in range(j * heads // NY, (j + 1) * heads // NY)
            ],
            axis=1,
        )
    for k in range(1, NY):
        to = (y + k) % NY
        send(lsend.at[to], lrecv.at[y], l_ss, l_rs, device(dy=k))
        send(tsend.at[to, pl.ds(0, 1), :], trecv.at[y, pl.ds(0, 1), :], t_ss, t_rs, device(dy=k))
    lrecv[y] = lsend[y]
    trecv[y] = tsend[y]

    logits = dot(cmat, bmat, ((1,), (1,)))
    cum_t = jnp.transpose(cum)
    dt_t = jnp.transpose(dt)
    for h in range(heads):
        span = slice(h * WIDTH, (h + 1) * WIDTH)
        decay = jnp.exp(jnp.where(mask, cum[:, h : h + 1] - cum_t[h : h + 1, :], -1e30))
        high, low = split(decay * logits * dt_t[h : h + 1, :])
        xh = x_ref[:, span]
        ybuf[:, span] = dot(high, xh) + dot(low, xh) + skip_ref[:, h : h + 1] * xh.astype(F32)
        gate = m_ref[:, span].astype(F32)
        smbuf[:, span] = gate / (1.0 + jnp.exp(-gate))

    arrived(lrecv.at[pl.ds(0, NY - 1)], l_rs)
    arrived(trecv.at[pl.ds(0, NY - 1), pl.ds(0, 1), :], t_rs)
    before = [jnp.zeros((1, pair), F32)]
    current = lrecv[0].astype(F32)
    for j in range(NY):
        before.append(before[-1] + trecv[j][0:1, :])
        if j:
            qbuf[j - 1] = current
            current = jnp.exp(trecv[j][0:1, :]) * current + lrecv[j].astype(F32)
    size = STATE // NZ
    for k in range(NZ):
        rsend[k] = current[k * size : (k + 1) * size, :].astype(BF16)
    dsend[...] = jnp.broadcast_to(before[NY], (8, pair))
    for k in (4, 3, 5, 2, 6, 1, 7):
        to = (z + k) % NZ
        send(rsend.at[to], rrecv.at[z], r_ss, r_rs, device(dz=k))
        send(dsend.at[pl.ds(0, 1), :], drecv.at[z, pl.ds(0, 1), :], d_ss, d_rs, device(dz=k))
    rrecv[z] = rsend[z]
    drecv[z] = dsend[...]
    relay(5)

    arrived(rrecv.at[pl.ds(0, NZ - 1)], r_rs)
    arrived(drecv.at[pl.ds(0, NZ - 1), pl.ds(0, 1), :], d_rs)
    current = jnp.zeros((size, pair), F32)
    for k in range(NZ):
        esend[k] = current.astype(BF16)
        current = jnp.exp(drecv[k][0:1, :]) * current + rrecv[k].astype(F32)
    for k in (4, 3, 5, 2, 6, 1, 7):
        to = (z + k) % NZ
        send(esend.at[to], erecv.at[z], e_ss, e_rs, device(dz=k))
    erecv[z] = esend[z]
    relay(8)
    arrived(erecv.at[pl.ds(0, NZ - 1)], e_rs)
    entry = jnp.concatenate([erecv[k].astype(F32) for k in range(NZ)], axis=0)
    ssend[0] = entry.astype(BF16)
    for j in range(1, NY):
        ssend[j] = (qbuf[j - 1] + jnp.exp(before[j]) * entry).astype(BF16)
    for k in range(1, NY):
        to = (y + k) % NY
        send(ssend.at[to], srecv.at[y], s_ss, s_rs, device(dy=k))
    srecv[y] = ssend[y]
    relay(11)
    arrived(srecv.at[pl.ds(0, NY - 1)], s_rs)

    grown = jnp.exp(cum)
    squares = jnp.zeros((tokens, WIDTH), F32)
    for j in range(NY):
        inter = dot(cmat, srecv[j])
        for i in range(heads // NY):
            h = j * heads // NY + i
            span = slice(h * WIDTH, (h + 1) * WIDTH)
            value = ybuf[:, span] + grown[:, h : h + 1] * inter[:, i * WIDTH : (i + 1) * WIDTH]
            value = value * smbuf[:, span]
            ybuf[:, span] = value
            squares = squares + value * value
    mean = jnp.sum(squares, axis=1, keepdims=True) * (1.0 / channels)
    scale = lax.rsqrt(mean + 1e-05)
    abuf[0] = (ybuf[...] * scale * gain_ref[...]).astype(BF16)

    turns = (0, -1, 1, 2)

    def a_part(turn, half):
        return abuf.at[turn, pl.ds(half * thalf, thalf), :]

    for i in range(2):
        for d, sign in enumerate((1, -1)):
            half = i if d == 0 else 1 - i
            send(
                a_part(0, half),
                a_part(1 + d, half),
                a_ss,
                a_rs.at[d, i],
                device(dy=sign),
            )

    distances = (0, 1, -1, 2, -2, 3, -3, 4)
    stages = ((0, 1), (1, 3), (3, 4))
    whole = (0, NY)

    def owner(n):
        origin = (z + distances[n]) % NZ
        return origin // NC, origin % NC

    def lanes_of(half):
        return pl.ds(0, cols) if half is None else pl.ds(half * chalf, chalf)

    def index_of(span, half):
        return (half or 0) if span == whole else stages.index(span)

    def partner_copy(n, span, half):
        rows = pl.ds(span[0], span[1] - span[0])
        index = index_of(span, half)
        return (
            part_sums.at[1 - core, n, rows, :, lanes_of(half)],
            precv.at[n, rows, :, lanes_of(half)],
            p_ss,
            p_rs.at[3 * n + index if n < 5 else 10 + n + index],
        )

    def multiply(n, span, half):
        origin = (z + distances[n]) % NZ
        if half is None:
            part = jnp.concatenate([wall[origin, 0], wall[origin, 1]], axis=1)
        else:
            part = wall[origin, half]
        width = part.shape[1]
        step = min(2, span[1] - span[0])
        for first in range(span[0], span[1], step):
            a = abuf[first : first + step].reshape(step * tokens, channels)
            total = dot(a, part).reshape(step, tokens, width)
            for c in range(NC):
                part_sums[c, n, first : first + step, :, lanes_of(half)] = total[
                    :, c * share : (c + 1) * share, :
                ]
        send(*partner_copy(n, span, half), device(dc=1))

    slab = share // NX

    def chip_sum(n, span, half):
        _, dst, _, rs = partner_copy(n, span, half)
        arrived(dst, rs)
        lanes = lanes_of(half)
        both = part_sums[core, n, span[0] : span[1], :, lanes]
        both = both + precv[n, span[0] : span[1], :, lanes]
        for j in range(NX):

            @pl.when(x == j)
            def _():
                xown[n, span[0] : span[1], :, lanes] = both[:, j * slab : (j + 1) * slab, :]

        both = both.astype(BF16)
        for j in range(NX):
            xsend[n, j, span[0] : span[1], :, lanes] = both[:, j * slab : (j + 1) * slab, :]
        rows = pl.ds(span[0], span[1] - span[0])
        for k in (2, 1, 3):
            send(
                xsend.at[n, (x + k) % NX, rows, :, lanes],
                xrecv.at[n, k - 1, rows, :, lanes],
                x_ss,
                x_rs.at[n],
                device(dx=k),
            )

    mine = pl.ds(pl.multiple_of(y * cols, cols), cols)
    place = pl.ds(pl.multiple_of(core * share + x * slab, slab), slab)

    def finish(n):
        value = xown[n]
        arrived(xrecv.at[n], x_rs.at[n])
        for k in range(1, NX):
            value = value + xrecv[n, k - 1].astype(F32)
        fsend[n] = value.astype(BF16)
        to_x, to_core = owner(n)
        for t in (3, 1, 2):
            to = (z * NY + (y + turns[t]) % NY, to_x * NC + to_core)
            send(fsend.at[n, t], out_ref.at[place, mine], f_ss, f_rs, to)
        own = (to_x == x) & (to_core == core)

        @pl.when(own)
        def _():
            pltpu.make_async_copy(fsend.at[n, 0], out_ref.at[place, mine], f_rs).start()

        @pl.when(jnp.logical_not(own))
        def _():
            send(
                fsend.at[n, 0], out_ref.at[place, mine], o_ss, f_rs, (seq, to_x * NC + to_core)
            )

    pending = []

    def unit(n, span, half=None):
        multiply(n, span, half)
        pending.append((n, span, half))
        if len(pending) > 1:
            chip_sum(*pending.pop(0))

    relay(11)
    for n in range(3):
        unit(n, stages[0])
    relay(12)
    for d, sign in enumerate((1, -1)):
        arrived(a_part(1 + d, d), a_rs.at[d, 0])
        send(a_part(1 + d, d), a_part(3, d), a_ss, a_rs.at[d, 2], device(dy=sign))
    relay(13)
    for n in range(3, 5):
        unit(n, stages[0])
    for d in range(2):
        arrived(a_part(1 + d, 1 - d), a_rs.at[d, 1])
    for n in range(5):
        unit(n, stages[1])
    relay(15)
    sent(lsend.at[pl.ds(0, NY - 1)], l_ss)
    sent(tsend.at[pl.ds(0, NY - 1), pl.ds(0, 1), :], t_ss)
    sent(rsend.at[pl.ds(0, NZ - 1)], r_ss)
    sent(drecv.at[pl.ds(0, NZ - 1), pl.ds(0, 1), :], d_ss)
    sent(esend.at[pl.ds(0, NZ - 1)], e_ss)
    sent(ssend.at[pl.ds(0, NY - 1)], s_ss)
    for d in range(2):
        arrived(a_part(3, d), a_rs.at[d, 2])
    for n in range(5):
        unit(n, stages[2])
    relay(16)
    unit(5, whole)
    unit(6, whole)
    sent(abuf.at[pl.ds(0, 3)], a_ss)
    relay(17)
    unit(7, whole, 0)
    relay(18)
    unit(7, whole, 1)
    chip_sum(*pending.pop(0))
    for n in range(NZ - 1):
        finish(n)
    finish(NZ - 1)

    sent(wall.at[pl.ds(0, NZ - 1)], w_ss)
    sent(precv, p_ss)
    sent(xrecv, x_ss)
    arrived(out_ref, f_rs)
    sent(fsend.at[:, pl.ds(1, NY - 1)], f_ss)
    sent(fsend.at[pl.ds(0, NZ - 1), 0], o_ss)


def shards(
    x_in, multiplier_channels, b_proj, c_proj, dt_raw, dt_bias, a_log, skip_d, norm_gain, w_out
):
    tokens, channels = x_in.shape
    depth, cols = w_out.shape
    pair = channels // NY
    size = STATE // NZ
    vmem = pl.BlockSpec(memory_space=pltpu.VMEM)
    dma = pltpu.SemaphoreType.DMA
    half = cols // 2
    share = tokens // NC
    heads = channels // WIDTH
    scratch = [
        pltpu.VMEM((heads, tokens), F32),
        pltpu.VMEM((1, heads), F32),
        pltpu.VMEM((1, heads), F32),
        pltpu.VMEM((1, heads), F32),
        pltpu.VMEM((1, channels), F32),
        pltpu.VMEM((tokens, STATE), BF16),
        pltpu.VMEM((tokens, STATE), BF16),
        pltpu.VMEM((tokens, channels), BF16),
        pltpu.VMEM((tokens, channels), BF16),
        pltpu.VMEM((NZ, 2, depth, half), BF16),
        pltpu.VMEM((NY, tokens, channels), BF16),
        pltpu.VMEM((tokens, channels), F32),
        pltpu.VMEM((tokens, channels), F32),
        pltpu.VMEM((NY - 1, STATE, pair), F32),
        pltpu.VMEM((NY, STATE, pair), BF16),
        pltpu.VMEM((NY, STATE, pair), BF16),
        pltpu.VMEM((NY, 8, pair), F32),
        pltpu.VMEM((NY, 8, pair), F32),
        pltpu.VMEM((NZ, size, pair), BF16),
        pltpu.VMEM((NZ, size, pair), BF16),
        pltpu.VMEM((8, pair), F32),
        pltpu.VMEM((NZ, 8, pair), F32),
        pltpu.VMEM((NZ, size, pair), BF16),
        pltpu.VMEM((NZ, size, pair), BF16),
        pltpu.VMEM((NY, STATE, pair), BF16),
        pltpu.VMEM((NY, STATE, pair), BF16),
        pltpu.VMEM((NC, NZ, NY, share, cols), F32),
        pltpu.VMEM((NZ, NY, share, cols), F32),
        pltpu.VMEM((NZ, NX, NY, share // NX, cols), BF16),
        pltpu.VMEM((NZ, NY, share // NX, cols), F32),
        pltpu.VMEM((NZ, NX - 1, NY, share // NX, cols), BF16),
        pltpu.VMEM((NZ, NY, share // NX, cols), BF16),
        dma((9,)),
        dma((2,)),
        dma, dma((2, 14)),
        dma, dma, dma, dma,
        dma, dma, dma, dma,
        dma, dma,
        dma, dma,
        dma, dma((2, 3)),
        dma, dma((19,)),
        dma, dma((NZ,)),
        dma, dma, dma,
    ]
    return pl.pallas_call(
        kernel,
        out_shape=pltpu.VMEM((tokens, channels), BF16),
        in_specs=[pl.BlockSpec(memory_space=pl.ANY)] * 10,
        out_specs=vmem,
        scratch_shapes=scratch,
        compiler_params=pltpu.CompilerParams(
            collective_id=0, has_side_effects=True, vmem_limit_bytes=56 * 1024 * 1024
        ),
        name="mixer",
    )(
        dt_raw.T,
        dt_bias.reshape(1, -1),
        a_log.reshape(1, -1),
        skip_d.reshape(1, -1),
        norm_gain.reshape(1, -1),
        b_proj,
        c_proj,
        x_in,
        multiplier_channels,
        w_out,
    )


def solution(mesh):
    return jax.shard_map(
        shards,
        mesh=mesh,
        in_specs=(
            P("seq", "grp"),
            P("seq", "grp"),
            P("seq", "grp"),
            P("seq", "grp"),
            P("seq", "grp"),
            P("grp"),
            P("grp"),
            P("grp"),
            P("grp"),
            P("grp", "seq"),
        ),
        out_specs=P("seq", "grp"),
        check_vma=False,
    )
```
